32 devices in a mesh: vid: 2 (over x), tm: 16 (over z, y, core).
Axes of the slice: x: 2, y: 2, z: 4, core: 2. Of those that a mesh axis runs over, the one named last changes fastest.
Arguments:
- queries: bfloat16 [4096, 1536], P(('vid', 'tm')), parts along dimension 0, may hold values from -6 to 6
- keys: bfloat16 [4096, 1536], P(('vid', 'tm')), parts along dimension 0, may hold values from -6 to 6
- values: bfloat16 [4096, 1536], P(('vid', 'tm')), parts along dimension 0, may hold values from -6 to 6
- far_picks: int32 [64, 8], P(('vid', 'tm')), parts along dimension 0, may hold values from 0 to 1
- out_weight: bfloat16 [1536, 1536], replicated, may hold values from -0.15625 to 0.15625
Outputs:
- mixed: bfloat16 [4096, 1536], P(('vid', 'tm')), parts along dimension 0
The draws below stay inside these ranges and needn't reach their ends.
There are 2 independent parts, one for each index of `vid`. The reference program is written for one: setup_inputs(seed, part) draws one part's arguments, and reference() takes and returns one part's arrays. A program takes and returns all parts, laid end to end along the dimension named above; an argument that names none is the same for every part. Nothing has to cross between parts.
All inputs are finite; a program needn't handle non-finite values.
Results may differ from the reference program's by a relative error of at most 0.0056.
Values may be sent and summed in bfloat16 or wider, within the bound.
A program may use at most 64 MiB of HBM per device.

```python
import jax
import jax.numpy as jnp
from jax import lax

D = 1536
HEADS = 12
HEAD_DIM = 128
BLK = 64
LEVELS = 2
PICKS = 2
TOK_DEV = 128
FAR = 8
NB_DEV = 2
TOKENS = 2048
N_TM = 16


def paired_draw(key):
    base_key = jax.random.fold_in(key, 101)
    first_key, second_key = jax.random.split(base_key, 2)
    full_shape = (TOKENS, D)
    query_raw = jnp.clip(jax.random.normal(first_key, full_shape, jnp.float32), -5.0, 5.0)
    key_raw = jnp.clip(jax.random.normal(second_key, full_shape, jnp.float32), -5.0, 5.0)
    return (jnp.clip(query_raw, -6.0, 6.0), jnp.clip(key_raw, -6.0, 6.0))


def draw_queries(key, part):
    return paired_draw(key)[0].astype(jnp.bfloat16)


def draw_keys(key, part):
    return paired_draw(key)[1].astype(jnp.bfloat16)


def place_ends(drawn, own_key, low, high):
    longest = drawn.shape.index(max(drawn.shape))
    spots = []
    for shift in (0, 1):
        where = [jax.random.randint(jax.random.fold_in(own_key, axis), (), 0, length) for axis, length in enumerate(drawn.shape)]
        where[longest] = (where[longest] + shift) % drawn.shape[longest]
        spots.append(tuple(where))
    return drawn.at[spots[0]].set(low).at[spots[1]].set(high)


def levels(key, extent, cuts, smallest, largest):
    level = 1.0
    for axis_at, parts in cuts:
        draws = jax.random.uniform(jax.random.fold_in(jax.random.fold_in(key, 6), axis_at), (parts,), jnp.float32, smallest / len(cuts), largest / len(cuts))
        level = level * jnp.repeat(jnp.exp(draws), extent[axis_at] // parts).reshape((-1,) + (1,) * (len(extent) - 1 - axis_at))
    return level


def centred(key, extent, scale, reach, cuts=(), kind=jnp.bfloat16):
    drawn = scale * jax.random.normal(key, extent, jnp.float32)
    if cuts:
        drawn = drawn * levels(key, extent, cuts, -0.22, 0.18)
    return jnp.clip(drawn, -reach, reach).astype(kind)


def setup_inputs(seed: int = 0, part: int = 0) -> dict:
    key_of = jax.random.split(jax.random.key(seed), 6)
    own_keys = jax.random.split(jax.random.fold_in(key_of[5], part), 6)
    queries = draw_queries(jax.random.fold_in(jax.random.fold_in(key_of[5], part), 71), part)
    keys = draw_keys(jax.random.fold_in(jax.random.fold_in(key_of[5], part), 71), part)
    values = centred(own_keys[2], (TOKENS, D), 1.0, 6.0, ((0, 16),))
    far_picks = place_ends(jax.random.randint(own_keys[3], (TOKENS // BLK, FAR), 0, NB_DEV), jax.random.fold_in(own_keys[3], 1), 0, NB_DEV - 1).astype(jnp.int32)
    out_weight = centred(key_of[4], (D, D), D ** -0.5, 0.15625)
    return {"queries": queries, "keys": keys, "values": values, "far_picks": far_picks, "out_weight": out_weight}


def far_offsets():
    offset_list = []
    for column in range(FAR):
        magnitude = 2 ** (1 + (column // PICKS) % LEVELS)
        offset_list.append(-magnitude if column < FAR // 2 else magnitude)
    return offset_list


def attend(query_rows, near_pair, near_valid, far_pair, far_valid, out_weight):
    blocks = query_rows.shape[0] // BLK
    scale = HEAD_DIM ** -0.5
    query_heads = query_rows.reshape(blocks, BLK, HEADS, HEAD_DIM).astype(jnp.float32)
    near_keys = near_pair[0].reshape(-1, HEADS, HEAD_DIM).astype(jnp.float32)
    near_values = near_pair[1].reshape(-1, HEADS, HEAD_DIM).astype(jnp.float32)
    far_keys = far_pair[0].reshape(blocks, -1, HEADS, HEAD_DIM).astype(jnp.float32)
    far_values = far_pair[1].reshape(blocks, -1, HEADS, HEAD_DIM).astype(jnp.float32)
    near_scores = jnp.einsum("bqhd,khd->bhqk", query_heads, near_keys) * scale
    near_scores = jnp.where(near_valid, near_scores, jnp.float32(-1e30))
    far_scores = jnp.einsum("bqhd,bkhd->bhqk", query_heads, far_keys) * scale
    far_scores = jnp.where(far_valid, far_scores, jnp.float32(-1e30))
    top_score = jnp.maximum(jnp.max(near_scores, -1), jnp.max(far_scores, -1))[..., None]
    near_exp = jnp.exp(near_scores - top_score)
    far_exp = jnp.exp(far_scores - top_score)
    total = jnp.sum(near_exp, -1) + jnp.sum(far_exp, -1)
    near_weights = lax.optimization_barrier(near_exp.astype(jnp.bfloat16)).astype(jnp.float32)
    far_weights = lax.optimization_barrier(far_exp.astype(jnp.bfloat16)).astype(jnp.float32)
    summed = jnp.einsum("bhqk,khd->bqhd", near_weights, near_values)
    summed = summed + jnp.einsum("bhqk,bkhd->bqhd", far_weights, far_values)
    attended = (summed / jnp.transpose(total, (0, 2, 1))[..., None]).reshape(blocks * BLK, D).astype(jnp.bfloat16)
    return jnp.dot(attended, out_weight, preferred_element_type=jnp.float32).astype(jnp.bfloat16)


def reference(queries, keys, values, far_picks, out_weight):
    blocks = TOK_DEV // BLK
    pair = jnp.stack([keys, values])
    padded = jnp.pad(pair, ((0, 0), (TOK_DEV, TOK_DEV), (0, 0)))
    offset_list = far_offsets()

    def one_device(device):
        start = (device * TOK_DEV).astype(jnp.int32)
        query_rows = lax.dynamic_slice_in_dim(queries, start, TOK_DEV, 0)
        near_pair = lax.dynamic_slice_in_dim(padded, start, 3 * TOK_DEV, 1)
        picks = lax.dynamic_slice_in_dim(far_picks, (device * blocks).astype(jnp.int32), blocks, 0)
        chosen_list = []
        valid_list = []
        for column in range(FAR):
            source = device + offset_list[column]
            usable = (source >= 0) & (source < N_TM)
            source_start = (jnp.clip(source, 0, N_TM - 1) * TOK_DEV).astype(jnp.int32)
            shard = lax.dynamic_slice_in_dim(pair, source_start, TOK_DEV, 1).reshape(2, blocks, BLK, D)
            chosen_list.append(jnp.take(shard, picks[:, column], axis=1))
            valid_list.append(usable)
        far_pair = jnp.stack(chosen_list, 2).reshape(2, blocks, FAR * BLK, D)
        far_valid = jnp.repeat(jnp.stack(valid_list), BLK)
        near_valid = jnp.repeat(jnp.stack([device > 0, jnp.array(True), device < N_TM - 1]), TOK_DEV)
        return attend(query_rows, near_pair, near_valid, far_pair, far_valid, out_weight)

    result = lax.map(one_device, jnp.arange(N_TM, dtype=jnp.int32))
    return result.reshape(TOKENS, D)
```

```python
import functools
import math

import jax
import jax.numpy as jnp
from jax import lax
from jax.experimental import pallas as pl
from jax.experimental.pallas import tpu as pltpu
from jax.sharding import PartitionSpec as P

HEADS = 12
HEAD_DIM = 128
BLK = 64
NEG = -1e30
EXP_SCALE = HEAD_DIM ** (-0.5) * math.log2(math.e)
XF, SIB, OWN, ZP, ZM = range(5)
TO_ZP, TO_ZM, HAND = range(3)
F_ZP, F_ZM, F_OWN, F_ZPY, F_NEAR = range(5)
MESH = pl.DeviceIdType.MESH
GROUPS = (2, 2, 2, 2, 2, 2)
FIRST = tuple(sum(GROUPS[:g]) for g in range(len(GROUPS)))
LAG = 3


def kernel(
    devices,
    picks_hbm,
    q_hbm,
    k_hbm,
    v_hbm,
    w_hbm,
    out,
    picks,
    picks_y,
    qv,
    qy,
    wv,
    kbuf,
    vbuf,
    mult,
    top,
    tot,
    acc,
    give_o,
    give_l,
    take_o,
    take_l,
    mixed_heads,
    load_sem,
    send_z,
    recv_z,
    send_sib,
    recv_sib,
    send_y,
    recv_y,
    send_p,
    recv_p,
):
    rows = q_hbm.shape[0]
    chips = devices // 2
    count = len(GROUPS)
    p = lax.axis_index("tm")
    chip = p // 2
    core = p % 2
    even = chip % 2 == 0
    step = jnp.where(even, 1, -1)
    has_p = (chip + 2 * step >= 0) & (chip + 2 * step < chips)
    has_m = (chip - 2 * step >= 0) & (chip - 2 * step < chips)
    gives = (core + chip) % 2 == 0
    takes = jnp.logical_not(gives)

    sib = p + 1 - 2 * core
    y_dev = p + 2 * step
    zp_dev = p + 4 * step
    zm_dev = p - 4 * step
    bufs = (kbuf, vbuf)
    hbms = (k_hbm, v_hbm)

    def columns_of(g):
        return pl.ds(FIRST[g] * HEAD_DIM, GROUPS[g] * HEAD_DIM)

    def slot(index):
        return pl.ds(index * rows, rows)

    def remote(src, dst, send, recv, dev):
        return pltpu.make_async_remote_copy(
            src_ref=src, dst_ref=dst, send_sem=send, recv_sem=recv, device_id={"tm": dev}, device_id_type=MESH
        )

    def along_z(kind, g, kv):
        dst, dev = ((ZM, zp_dev), (ZP, zm_dev), (XF, sib))[kind]
        columns = columns_of(g)
        src = bufs[kv].at[slot(ZP), columns] if kind == HAND else hbms[kv].at[:, columns]
        where = (kind, g, kv)
        return remote(src, bufs[kv].at[slot(dst), columns], send_z.at[where], recv_z.at[where], dev)

    def to_sib(kv):
        return remote(hbms[kv], bufs[kv].at[slot(SIB)], send_sib.at[kv], recv_sib.at[kv], sib)

    def to_y(kind, g):
        columns = columns_of(g)
        src, dst = (
            (q_hbm.at[:, columns], qy.at[:, columns]),
            (give_o.at[:, columns], take_o.at[:, columns]),
            (give_l.at[g], take_l.at[g]),
        )[kind]
        return remote(src, dst, send_y.at[kind, g], recv_y.at[kind, g], y_dev)

    picks_to_y = remote(picks_hbm, picks_y, send_p, recv_p, y_dev)
    load_w = pltpu.make_async_copy(w_hbm, wv, load_sem.at[4])
    load_picks = pltpu.make_async_copy(picks_hbm, picks, load_sem.at[3])
    load_picks.start()
    loads = [
        pltpu.make_async_copy(q_hbm, qv, load_sem.at[0]),
        pltpu.make_async_copy(k_hbm, kbuf.at[slot(OWN)], load_sem.at[1]),
        pltpu.make_async_copy(v_hbm, vbuf.at[slot(OWN)], load_sem.at[2]),
    ]
    for load in loads:
        load.start()

    barrier = pltpu.get_barrier_semaphore()

    def greet(dev):
        pl.semaphore_signal(barrier, inc=1, device_id={"tm": dev}, device_id_type=MESH)

    greet(sib)
    greet(y_dev)

    @pl.when(has_p)
    def _():
        greet(zp_dev)

    @pl.when(has_m)
    def _():
        greet(zm_dev)

    pl.semaphore_wait(barrier, 2 + jnp.where(has_p, 1, 0) + jnp.where(has_m, 1, 0))

    def send_group(g):
        @pl.when(has_m)
        def _():
            for kv in range(2):
                along_z(TO_ZM, g, kv).start()

        to_y(0, g).start()

        @pl.when(has_p)
        def _():
            for kv in range(2):
                along_z(TO_ZP, g, kv).start()

    picks_to_y.start()
    send_group(0)
    for kv in range(2):
        to_sib(kv).start()
    for g in range(1, count):
        send_group(g)

    load_w.start()
    load_picks.wait()
    picks_to_y.wait_recv()

    ints = jnp.int32
    row_at = lax.broadcasted_iota(ints, (rows, rows), 0)
    col_at = lax.broadcasted_iota(ints, (rows, rows), 1)
    row_first = row_at < BLK
    col_first = col_at < BLK
    diagonal = row_at == col_at

    def fill(index, named, up, down, valid):
        one = jnp.where(valid, 1, 0)
        seconds = [
            jnp.where(even, named[b, up] + named[b, up + 1], named[b, down] + named[b, down + 1]) for b in range(2)
        ]
        cells = [[((2 - n) * one).astype(jnp.float32), (n * one).astype(jnp.float32)] for n in seconds]
        mult[index] = jnp.where(
            row_first,
            jnp.where(col_first, cells[0][0], cells[0][1]),
            jnp.where(col_first, cells[1][0], cells[1][1]),
        )

    near_valid = gives | has_p
    fill(F_ZP, picks, 6, 2, has_p)
    fill(F_ZM, picks, 2, 6, has_m)
    fill(F_OWN, picks_y, 0, 4, True)
    fill(F_ZPY, picks_y, 4, 0, has_p)
    mult[F_NEAR] = jnp.full((rows, rows), jnp.where(near_valid, 1.0, 0.0), jnp.float32)

    def clear(index):
        vbuf[index * rows : (index + 1) * rows] = jnp.zeros((rows, vbuf.shape[1]), vbuf.dtype)

    @pl.when(jnp.logical_not(has_p))
    def _():
        clear(ZP)

    @pl.when(jnp.logical_not(has_m))
    def _():
        clear(ZM)

    @pl.when(jnp.logical_not(near_valid))
    def _():
        clear(XF)

    near = pl.ds(pl.multiple_of(jnp.where(gives, SIB, XF) * rows, rows), rows)

    def attend(query, head, parts):
        columns = slice(head * HEAD_DIM, (head + 1) * HEAD_DIM)
        pieces = []
        for where, factors in parts:
            scores = lax.dot_general(
                query[:, columns],
                kbuf[where, columns],
                (((1,), (1,)), ((), ())),
                preferred_element_type=jnp.float32,
            )
            for i, factor in enumerate(factors):
                piece = scores[:, i * rows : (i + 1) * rows]
                if factor is not None:
                    piece = jnp.where(mult[factor] > 0, piece, NEG)
                pieces.append((piece, factor))
        high = functools.reduce(jnp.maximum, [piece for piece, _ in pieces])
        high = jnp.broadcast_to(jnp.max(high, axis=1, keepdims=True), high.shape)
        weights = []
        for piece, factor in pieces:
            weight = jnp.exp2((piece - high) * EXP_SCALE)
            if factor is not None:
                weight = weight * mult[factor]
            weights.append(weight)
        summed = functools.reduce(jnp.add, weights)
        summed = jnp.broadcast_to(jnp.sum(summed, axis=1, keepdims=True), summed.shape)
        mixed = None
        for where, factors in parts:
            now, weights = weights[: len(factors)], weights[len(factors) :]
            now = jnp.concatenate([w.astype(jnp.bfloat16) for w in now], axis=1)
            term = jnp.dot(now, vbuf[where, columns], preferred_element_type=jnp.float32)
            mixed = term if mixed is None else mixed + term
        return high * EXP_SCALE, summed, mixed

    def help_group(g):
        for j in range(GROUPS[g]):
            head = FIRST[g] + j
            columns = slice(head * HEAD_DIM, (head + 1) * HEAD_DIM)
            high, summed, mixed = attend(
                qy, head, ((near, (F_NEAR,)), (slice(OWN * rows, (ZP + 1) * rows), (F_OWN, F_ZPY)))
            )
            give_o[:, columns] = (mixed / summed).astype(give_o.dtype)
            size = high + jnp.log2(summed)
            give_l[g, j : j + 1] = jnp.sum(jnp.where(diagonal, size, 0.0), axis=0, keepdims=True)

    def local_group(g):
        for j in range(GROUPS[g]):
            head = FIRST[g] + j
            top[head], tot[head], acc[head] = attend(
                qv, head, ((slice(SIB * rows, (ZM + 1) * rows), (None, None, F_ZP, F_ZM)),)
            )

    def merge_group(g):
        for kind in (1, 2):
            to_y(kind, g).wait_recv()
        for j in range(GROUPS[g]):
            head = FIRST[g] + j
            columns = slice(head * HEAD_DIM, (head + 1) * HEAD_DIM)
            size = jnp.broadcast_to(take_l[g, j : j + 1], (rows, rows))
            size = jnp.sum(jnp.where(diagonal, size, 0.0), axis=1, keepdims=True)
            size = jnp.broadcast_to(size, (rows, rows))
            high = jnp.maximum(top[head], size)
            mine = jnp.exp2(top[head] - high)
            theirs = jnp.exp2(size - high)
            mixed = acc[head] * mine + take_o[:, columns].astype(jnp.float32) * theirs
            mixed_heads[:, columns] = (mixed / (tot[head] * mine + theirs)).astype(mixed_heads.dtype)

    for load in loads:
        load.wait()
    for kv in range(2):
        to_sib(kv).wait_recv()

    for g in range(count):

        @pl.when(has_p)
        def _():
            for kv in range(2):
                along_z(TO_ZM, g, kv).wait_recv()

        @pl.when(has_p & gives)
        def _():
            for kv in range(2):
                along_z(HAND, g, kv).start()

        to_y(0, g).wait_recv()

        @pl.when(has_p & takes)
        def _():
            for kv in range(2):
                along_z(HAND, g, kv).wait_recv()

        help_group(g)
        for kind in (1, 2):
            to_y(kind, g).start()

        @pl.when(has_m)
        def _():
            for kv in range(2):
                along_z(TO_ZP, g, kv).wait_recv()

        local_group(g)
        if g >= LAG:
            merge_group(g - LAG)

    load_w.wait()
    for g in range(count - LAG, count - 1):
        merge_group(g)
    early = FIRST[-1] * HEAD_DIM
    projected = jnp.dot(mixed_heads[:, :early], wv[:early], preferred_element_type=jnp.float32)
    merge_group(count - 1)
    projected = projected + jnp.dot(mixed_heads[:, early:], wv[early:], preferred_element_type=jnp.float32)
    out[...] = projected.astype(out.dtype)

    picks_to_y.wait_send()
    for kv in range(2):
        to_sib(kv).wait_send()
    for g in range(count):
        for kind in range(3):
            to_y(kind, g).wait_send()

    @pl.when(has_p)
    def _():
        for g in range(count):
            for kv in range(2):
                along_z(TO_ZP, g, kv).wait_send()

    @pl.when(has_m)
    def _():
        for g in range(count):
            for kv in range(2):
                along_z(TO_ZM, g, kv).wait_send()

    @pl.when(has_p & gives)
    def _():
        for g in range(count):
            for kv in range(2):
                along_z(HAND, g, kv).wait_send()


def attention(devices, queries, keys, values, far_picks, out_weight):
    rows, width = queries.shape
    count = len(GROUPS)
    in_hbm = pl.BlockSpec(memory_space=pltpu.HBM)
    per_head = pltpu.VMEM((HEADS, rows, HEAD_DIM), jnp.float32)
    wide = pltpu.VMEM((rows, width), jnp.bfloat16)
    sizes = pltpu.VMEM((count, 8, rows), jnp.float32)
    dma = pltpu.SemaphoreType.DMA
    return pl.pallas_call(
        functools.partial(kernel, devices),
        out_shape=jax.ShapeDtypeStruct((rows, width), jnp.bfloat16),
        in_specs=[in_hbm] * 5,
        out_specs=pl.BlockSpec(memory_space=pltpu.VMEM),
        scratch_shapes=[
            pltpu.SMEM(far_picks.shape, jnp.int32),
            pltpu.SMEM(far_picks.shape, jnp.int32),
            wide,
            wide,
            pltpu.VMEM(out_weight.shape, jnp.bfloat16),
            pltpu.VMEM((5 * rows, width), jnp.bfloat16),
            pltpu.VMEM((5 * rows, width), jnp.bfloat16),
            pltpu.VMEM((5, rows, rows), jnp.float32),
            per_head,
            per_head,
            per_head,
            wide,
            sizes,
            wide,
            sizes,
            wide,
            dma((5,)),
            dma((3, count, 2)),
            dma((3, count, 2)),
            dma((2,)),
            dma((2,)),
            dma((3, count)),
            dma((3, count)),
            dma,
            dma,
        ],
        compiler_params=pltpu.CompilerParams(
            collective_id=0, has_side_effects=True, vmem_limit_bytes=67_000_000
        ),
        name="helper_attention",
    )(far_picks, queries, keys, values, out_weight)


def solution(mesh):
    devices = mesh.shape["tm"]

    def body(queries, keys, values, far_picks, out_weight):
        return attention(devices, queries, keys, values, far_picks, out_weight)

    placed = (
        P(("vid", "tm"), None),
        P(("vid", "tm"), None),
        P(("vid", "tm"), None),
        P(("vid", "tm"), None),
        P(),
    )
    return jax.shard_map(
        body, mesh=mesh, in_specs=placed, out_specs=P(("vid", "tm"), None), check_vma=False
    )
```

```python
import functools
import math

import jax
import jax.numpy as jnp
from jax import lax
from jax.experimental import pallas as pl
from jax.experimental.pallas import tpu as pltpu
from jax.sharding import PartitionSpec as P

HEADS = 12
HEAD_DIM = 128
BLK = 64
NEG = -1e30
EXP_SCALE = HEAD_DIM ** (-0.5) * math.log2(math.e)
XF, SIB, OWN, ZP, ZM = range(5)
TO_ZP, TO_ZM, HAND = range(3)
F_ZP, F_ZM, F_OWN, F_ZPY, F_NEAR = range(5)
MESH = pl.DeviceIdType.MESH
GROUPS = (3, 3, 3, 3)
FIRST = tuple(sum(GROUPS[:g]) for g in range(len(GROUPS)))
LAG = 3


def kernel(
    devices,
    picks_hbm,
    q_hbm,
    k_hbm,
    v_hbm,
    w_hbm,
    out,
    picks,
    picks_y,
    qv,
    qy,
    wv,
    kbuf,
    vbuf,
    mult,
    top,
    tot,
    acc,
    give_o,
    give_l,
    take_o,
    take_l,
    mixed_heads,
    load_sem,
    send_z,
    recv_z,
    send_sib,
    recv_sib,
    send_y,
    recv_y,
    send_p,
    recv_p,
):
    rows = q_hbm.shape[0]
    chips = devices // 2
    count = len(GROUPS)
    p = lax.axis_index("tm")
    chip = p // 2
    core = p % 2
    even = chip % 2 == 0
    step = jnp.where(even, 1, -1)
    has_p = (chip + 2 * step >= 0) & (chip + 2 * step < chips)
    has_m = (chip - 2 * step >= 0) & (chip - 2 * step < chips)
    gives = (core + chip) % 2 == 0
    takes = jnp.logical_not(gives)

    sib = p + 1 - 2 * core
    y_dev = p + 2 * step
    zp_dev = p + 4 * step
    zm_dev = p - 4 * step
    bufs = (kbuf, vbuf)
    hbms = (k_hbm, v_hbm)

    def columns_of(g):
        return pl.ds(FIRST[g] * HEAD_DIM, GROUPS[g] * HEAD_DIM)

    def slot(index):
        return pl.ds(index * rows, rows)

    def remote(src, dst, send, recv, dev):
        return pltpu.make_async_remote_copy(
            src_ref=src, dst_ref=dst, send_sem=send, recv_sem=recv, device_id={"tm": dev}, device_id_type=MESH
        )

    def along_z(kind, g, kv):
        dst, dev = ((ZM, zp_dev), (ZP, zm_dev), (XF, sib))[kind]
        columns = columns_of(g)
        src = bufs[kv].at[slot(ZP), columns] if kind == HAND else hbms[kv].at[:, columns]
        where = (kind, g, kv)
        return remote(src, bufs[kv].at[slot(dst), columns], send_z.at[where], recv_z.at[where], dev)

    def to_sib(kv):
        return remote(hbms[kv], bufs[kv].at[slot(SIB)], send_sib.at[kv], recv_sib.at[kv], sib)

    def to_y(kind, g):
        columns = columns_of(g)
        src, dst = (
            (q_hbm.at[:, columns], qy.at[:, columns]),
            (give_o.at[:, columns], take_o.at[:, columns]),
            (give_l.at[g], take_l.at[g]),
        )[kind]
        return remote(src, dst, send_y.at[kind, g], recv_y.at[kind, g], y_dev)

    picks_to_y = remote(picks_hbm, picks_y, send_p, recv_p, y_dev)
    load_w = pltpu.make_async_copy(w_hbm, wv, load_sem.at[4])
    load_picks = pltpu.make_async_copy(picks_hbm, picks, load_sem.at[3])
    load_picks.start()
    loads = [
        pltpu.make_async_copy(q_hbm, qv, load_sem.at[0]),
        pltpu.make_async_copy(k_hbm, kbuf.at[slot(OWN)], load_sem.at[1]),
        pltpu.make_async_copy(v_hbm, vbuf.at[slot(OWN)], load_sem.at[2]),
    ]
    for load in loads:
        load.start()

    barrier = pltpu.get_barrier_semaphore()

    def greet(dev):
        pl.semaphore_signal(barrier, inc=1, device_id={"tm": dev}, device_id_type=MESH)

    greet(sib)
    greet(y_dev)

    @pl.when(has_p)
    def _():
        greet(zp_dev)

    @pl.when(has_m)
    def _():
        greet(zm_dev)

    pl.semaphore_wait(barrier, 2 + jnp.where(has_p, 1, 0) + jnp.where(has_m, 1, 0))

    def send_group(g):
        @pl.when(has_m)
        def _():
            for kv in range(2):
                along_z(TO_ZM, g, kv).start()

        to_y(0, g).start()

        @pl.when(has_p)
        def _():
            for kv in range(2):
                along_z(TO_ZP, g, kv).start()

    picks_to_y.start()
    send_group(0)
    for kv in range(2):
        to_sib(kv).start()
    for g in range(1, count):
        send_group(g)

    load_w.start()
    load_picks.wait()
    picks_to_y.wait_recv()

    ints = jnp.int32
    row_at = lax.broadcasted_iota(ints, (rows, rows), 0)
    col_at = lax.broadcasted_iota(ints, (rows, rows), 1)
    row_first = row_at < BLK
    col_first = col_at < BLK
    diagonal = row_at == col_at

    def fill(index, named, up, down, valid):
        one = jnp.where(valid, 1, 0)
        seconds = [
            jnp.where(even, named[b, up] + named[b, up + 1], named[b, down] + named[b, down + 1]) for b in range(2)
        ]
        cells = [[((2 - n) * one).astype(jnp.float32), (n * one).astype(jnp.float32)] for n in seconds]
        mult[index] = jnp.where(
            row_first,
            jnp.where(col_first, cells[0][0], cells[0][1]),
            jnp.where(col_first, cells[1][0], cells[1][1]),
        )

    near_valid = gives | has_p
    fill(F_ZP, picks, 6, 2, has_p)
    fill(F_ZM, picks, 2, 6, has_m)
    fill(F_OWN, picks_y, 0, 4, True)
    fill(F_ZPY, picks_y, 4, 0, has_p)
    mult[F_NEAR] = jnp.full((rows, rows), jnp.where(near_valid, 1.0, 0.0), jnp.float32)

    def clear(index):
        vbuf[index * rows : (index + 1) * rows] = jnp.zeros((rows, vbuf.shape[1]), vbuf.dtype)

    @pl.when(jnp.logical_not(has_p))
    def _():
        clear(ZP)

    @pl.when(jnp.logical_not(has_m))
    def _():
        clear(ZM)

    @pl.when(jnp.logical_not(near_valid))
    def _():
        clear(XF)

    near = pl.ds(pl.multiple_of(jnp.where(gives, SIB, XF) * rows, rows), rows)

    def attend(query, head, parts):
        columns = slice(head * HEAD_DIM, (head + 1) * HEAD_DIM)
        pieces = []
        for where, factors in parts:
            scores = lax.dot_general(
                query[:, columns],
                kbuf[where, columns],
                (((1,), (1,)), ((), ())),
                preferred_element_type=jnp.float32,
            )
            for i, factor in enumerate(factors):
                piece = scores[:, i * rows : (i + 1) * rows]
                if factor is not None:
                    piece = jnp.where(mult[factor] > 0, piece, NEG)
                pieces.append((piece, factor))
        high = functools.reduce(jnp.maximum, [piece for piece, _ in pieces])
        high = jnp.broadcast_to(jnp.max(high, axis=1, keepdims=True), high.shape)
        weights = []
        for piece, factor in pieces:
            weight = jnp.exp2((piece - high) * EXP_SCALE)
            if factor is not None:
                weight = weight * mult[factor]
            weights.append(weight)
        summed = functools.reduce(jnp.add, weights)
        summed = jnp.broadcast_to(jnp.sum(summed, axis=1, keepdims=True), summed.shape)
        mixed = None
        for where, factors in parts:
            now, weights = weights[: len(factors)], weights[len(factors) :]
            now = jnp.concatenate([w.astype(jnp.bfloat16) for w in now], axis=1)
            term = jnp.dot(now, vbuf[where, columns], preferred_element_type=jnp.float32)
            mixed = term if mixed is None else mixed + term
        return high * EXP_SCALE, summed, mixed

    def help_group(g):
        for j in range(GROUPS[g]):
            head = FIRST[g] + j
            columns = slice(head * HEAD_DIM, (head + 1) * HEAD_DIM)
            high, summed, mixed = attend(
                qy, head, ((near, (F_NEAR,)), (slice(OWN * rows, (ZP + 1) * rows), (F_OWN, F_ZPY)))
            )
            give_o[:, columns] = (mixed / summed).astype(give_o.dtype)
            size = high + jnp.log2(summed)
            give_l[g, j : j + 1] = jnp.sum(jnp.where(diagonal, size, 0.0), axis=0, keepdims=True)

    def local_group(g):
        for j in range(GROUPS[g]):
            head = FIRST[g] + j
            top[head], tot[head], acc[head] = attend(
                qv, head, ((slice(SIB * rows, (ZM + 1) * rows), (None, None, F_ZP, F_ZM)),)
            )

    def merge_group(g):
        for kind in (1, 2):
            to_y(kind, g).wait_recv()
        for j in range(GROUPS[g]):
            head = FIRST[g] + j
            columns = slice(head * HEAD_DIM, (head + 1) * HEAD_DIM)
            size = jnp.broadcast_to(take_l[g, j : j + 1], (rows, rows))
            size = jnp.sum(jnp.where(diagonal, size, 0.0), axis=1, keepdims=True)
            size = jnp.broadcast_to(size, (rows, rows))
            high = jnp.maximum(top[head], size)
            mine = jnp.exp2(top[head] - high)
            theirs = jnp.exp2(size - high)
            mixed = acc[head] * mine + take_o[:, columns].astype(jnp.float32) * theirs
            mixed_heads[:, columns] = (mixed / (tot[head] * mine + theirs)).astype(mixed_heads.dtype)

    for load in loads:
        load.wait()
    for kv in range(2):
        to_sib(kv).wait_recv()

    for g in range(count):

        @pl.when(has_p)
        def _():
            for kv in range(2):
                along_z(TO_ZM, g, kv).wait_recv()

        @pl.when(has_p & gives)
        def _():
            for kv in range(2):
                along_z(HAND, g, kv).start()

        to_y(0, g).wait_recv()

        @pl.when(has_p & takes)
        def _():
            for kv in range(2):
                along_z(HAND, g, kv).wait_recv()

        help_group(g)
        for kind in (1, 2):
            to_y(kind, g).start()

        @pl.when(has_m)
        def _():
            for kv in range(2):
                along_z(TO_ZP, g, kv).wait_recv()

        local_group(g)
        if g >= LAG:
            merge_group(g - LAG)

    load_w.wait()
    for g in range(count - LAG, count - 1):
        merge_group(g)
    early = FIRST[-1] * HEAD_DIM
    projected = jnp.dot(mixed_heads[:, :early], wv[:early], preferred_element_type=jnp.float32)
    merge_group(count - 1)
    projected = projected + jnp.dot(mixed_heads[:, early:], wv[early:], preferred_element_type=jnp.float32)
    out[...] = projected.astype(out.dtype)

    picks_to_y.wait_send()
    for kv in range(2):
        to_sib(kv).wait_send()
    for g in range(count):
        for kind in range(3):
            to_y(kind, g).wait_send()

    @pl.when(has_p)
    def _():
        for g in range(count):
            for kv in range(2):
                along_z(TO_ZP, g, kv).wait_send()

    @pl.when(has_m)
    def _():
        for g in range(count):
            for kv in range(2):
                along_z(TO_ZM, g, kv).wait_send()

    @pl.when(has_p & gives)
    def _():
        for g in range(count):
            for kv in range(2):
                along_z(HAND, g, kv).wait_send()


def attention(devices, queries, keys, values, far_picks, out_weight):
    rows, width = queries.shape
    count = len(GROUPS)
    in_hbm = pl.BlockSpec(memory_space=pltpu.HBM)
    per_head = pltpu.VMEM((HEADS, rows, HEAD_DIM), jnp.float32)
    wide = pltpu.VMEM((rows, width), jnp.bfloat16)
    sizes = pltpu.VMEM((count, 8, rows), jnp.float32)
    dma = pltpu.SemaphoreType.DMA
    return pl.pallas_call(
        functools.partial(kernel, devices),
        out_shape=jax.ShapeDtypeStruct((rows, width), jnp.bfloat16),
        in_specs=[in_hbm] * 5,
        out_specs=pl.BlockSpec(memory_space=pltpu.VMEM),
        scratch_shapes=[
            pltpu.SMEM(far_picks.shape, jnp.int32),
            pltpu.SMEM(far_picks.shape, jnp.int32),
            wide,
            wide,
            pltpu.VMEM(out_weight.shape, jnp.bfloat16),
            pltpu.VMEM((5 * rows, width), jnp.bfloat16),
            pltpu.VMEM((5 * rows, width), jnp.bfloat16),
            pltpu.VMEM((5, rows, rows), jnp.float32),
            per_head,
            per_head,
            per_head,
            wide,
            sizes,
            wide,
            sizes,
            wide,
            dma((5,)),
            dma((3, count, 2)),
            dma((3, count, 2)),
            dma((2,)),
            dma((2,)),
            dma((3, count)),
            dma((3, count)),
            dma,
            dma,
        ],
        compiler_params=pltpu.CompilerParams(
            collective_id=0, has_side_effects=True, vmem_limit_bytes=56_000_000
        ),
        name="helper_attention",
    )(far_picks, queries, keys, values, out_weight)


def solution(mesh):
    devices = mesh.shape["tm"]

    def body(queries, keys, values, far_picks, out_weight):
        return attention(devices, queries, keys, values, far_picks, out_weight)

    placed = (
        P(("vid", "tm"), None),
        P(("vid", "tm"), None),
        P(("vid", "tm"), None),
        P(("vid", "tm"), None),
        P(),
    )
    return jax.shard_map(
        body, mesh=mesh, in_specs=placed, out_specs=P(("vid", "tm"), None), check_vma=False
    )
```

```python
import functools
import math

import jax
import jax.numpy as jnp
from jax import lax
from jax.experimental import pallas as pl
from jax.experimental.pallas import tpu as pltpu
from jax.sharding import PartitionSpec as P

HEADS = 12
HEAD_DIM = 128
BLK = 64
NEG = -1e30
EXP_SCALE = HEAD_DIM ** (-0.5) * math.log2(math.e)
XF, SIB, OWN, ZP, ZM = range(5)
TO_ZP, TO_ZM, HAND = range(3)
F_ZP, F_ZM, F_OWN, F_ZPY, F_NEAR = range(5)
MESH = pl.DeviceIdType.MESH
GROUPS = (4, 4, 2, 2)
FIRST = tuple(sum(GROUPS[:g]) for g in range(len(GROUPS)))
LAG = 3


def kernel(
    devices,
    picks_hbm,
    q_hbm,
    k_hbm,
    v_hbm,
    w_hbm,
    out,
    picks,
    picks_y,
    qv,
    qy,
    wv,
    kbuf,
    vbuf,
    mult,
    top,
    tot,
    acc,
    give_o,
    give_l,
    take_o,
    take_l,
    mixed_heads,
    load_sem,
    send_z,
    recv_z,
    send_sib,
    recv_sib,
    send_y,
    recv_y,
    send_p,
    recv_p,
):
    rows = q_hbm.shape[0]
    chips = devices // 2
    count = len(GROUPS)
    p = lax.axis_index("tm")
    chip = p // 2
    core = p % 2
    even = chip % 2 == 0
    step = jnp.where(even, 1, -1)
    has_p = (chip + 2 * step >= 0) & (chip + 2 * step < chips)
    has_m = (chip - 2 * step >= 0) & (chip - 2 * step < chips)
    gives = (core + chip) % 2 == 0
    takes = jnp.logical_not(gives)

    sib = p + 1 - 2 * core
    y_dev = p + 2 * step
    zp_dev = p + 4 * step
    zm_dev = p - 4 * step
    bufs = (kbuf, vbuf)
    hbms = (k_hbm, v_hbm)

    def columns_of(g):
        return pl.ds(FIRST[g] * HEAD_DIM, GROUPS[g] * HEAD_DIM)

    def slot(index):
        return pl.ds(index * rows, rows)

    def remote(src, dst, send, recv, dev):
        return pltpu.make_async_remote_copy(
            src_ref=src, dst_ref=dst, send_sem=send, recv_sem=recv, device_id={"tm": dev}, device_id_type=MESH
        )

    def along_z(kind, g, kv):
        dst, dev = ((ZM, zp_dev), (ZP, zm_dev), (XF, sib))[kind]
        columns = columns_of(g)
        src = bufs[kv].at[slot(ZP), columns] if kind == HAND else hbms[kv].at[:, columns]
        where = (kind, g, kv)
        return remote(src, bufs[kv].at[slot(dst), columns], send_z.at[where], recv_z.at[where], dev)

    def to_sib(kv):
        return remote(hbms[kv], bufs[kv].at[slot(SIB)], send_sib.at[kv], recv_sib.at[kv], sib)

    def to_y(kind, g):
        columns = columns_of(g)
        src, dst = (
            (q_hbm.at[:, columns], qy.at[:, columns]),
            (give_o.at[:, columns], take_o.at[:, columns]),
            (give_l.at[g], take_l.at[g]),
        )[kind]
        return remote(src, dst, send_y.at[kind, g], recv_y.at[kind, g], y_dev)

    picks_to_y = remote(picks_hbm, picks_y, send_p, recv_p, y_dev)
    load_w = pltpu.make_async_copy(w_hbm, wv, load_sem.at[4])
    load_picks = pltpu.make_async_copy(picks_hbm, picks, load_sem.at[3])
    load_picks.start()
    loads = [
        pltpu.make_async_copy(q_hbm, qv, load_sem.at[0]),
        pltpu.make_async_copy(k_hbm, kbuf.at[slot(OWN)], load_sem.at[1]),
        pltpu.make_async_copy(v_hbm, vbuf.at[slot(OWN)], load_sem.at[2]),
    ]
    for load in loads:
        load.start()

    barrier = pltpu.get_barrier_semaphore()

    def greet(dev):
        pl.semaphore_signal(barrier, inc=1, device_id={"tm": dev}, device_id_type=MESH)

    greet(sib)
    greet(y_dev)

    @pl.when(has_p)
    def _():
        greet(zp_dev)

    @pl.when(has_m)
    def _():
        greet(zm_dev)

    pl.semaphore_wait(barrier, 2 + jnp.where(has_p, 1, 0) + jnp.where(has_m, 1, 0))

    def send_group(g):
        @pl.when(has_m)
        def _():
            for kv in range(2):
                along_z(TO_ZM, g, kv).start()

        to_y(0, g).start()

        @pl.when(has_p)
        def _():
            for kv in range(2):
                along_z(TO_ZP, g, kv).start()

    picks_to_y.start()
    send_group(0)
    for kv in range(2):
        to_sib(kv).start()
    for g in range(1, count):
        send_group(g)

    load_w.start()
    load_picks.wait()
    picks_to_y.wait_recv()

    ints = jnp.int32
    row_at = lax.broadcasted_iota(ints, (rows, rows), 0)
    col_at = lax.broadcasted_iota(ints, (rows, rows), 1)
    row_first = row_at < BLK
    col_first = col_at < BLK
    diagonal = row_at == col_at

    def fill(index, named, up, down, valid):
        one = jnp.where(valid, 1, 0)
        seconds = [
            jnp.where(even, named[b, up] + named[b, up + 1], named[b, down] + named[b, down + 1]) for b in range(2)
        ]
        cells = [[((2 - n) * one).astype(jnp.float32), (n * one).astype(jnp.float32)] for n in seconds]
        mult[index] = jnp.where(
            row_first,
            jnp.where(col_first, cells[0][0], cells[0][1]),
            jnp.where(col_first, cells[1][0], cells[1][1]),
        )

    near_valid = gives | has_p
    fill(F_ZP, picks, 6, 2, has_p)
    fill(F_ZM, picks, 2, 6, has_m)
    fill(F_OWN, picks_y, 0, 4, True)
    fill(F_ZPY, picks_y, 4, 0, has_p)
    mult[F_NEAR] = jnp.full((rows, rows), jnp.where(near_valid, 1.0, 0.0), jnp.float32)

    def clear(index):
        vbuf[index * rows : (index + 1) * rows] = jnp.zeros((rows, vbuf.shape[1]), vbuf.dtype)

    @pl.when(jnp.logical_not(has_p))
    def _():
        clear(ZP)

    @pl.when(jnp.logical_not(has_m))
    def _():
        clear(ZM)

    @pl.when(jnp.logical_not(near_valid))
    def _():
        clear(XF)

    near = pl.ds(pl.multiple_of(jnp.where(gives, SIB, XF) * rows, rows), rows)

    def attend(query, head, parts):
        columns = slice(head * HEAD_DIM, (head + 1) * HEAD_DIM)
        pieces = []
        for where, factors in parts:
            scores = lax.dot_general(
                query[:, columns],
                kbuf[where, columns],
                (((1,), (1,)), ((), ())),
                preferred_element_type=jnp.float32,
            )
            for i, factor in enumerate(factors):
                piece = scores[:, i * rows : (i + 1) * rows]
                if factor is not None:
                    piece = jnp.where(mult[factor] > 0, piece, NEG)
                pieces.append((piece, factor))
        high = functools.reduce(jnp.maximum, [piece for piece, _ in pieces])
        high = jnp.broadcast_to(jnp.max(high, axis=1, keepdims=True), high.shape)
        weights = []
        for piece, factor in pieces:
            weight = jnp.exp2((piece - high) * EXP_SCALE)
            if factor is not None:
                weight = weight * mult[factor]
            weights.append(weight)
        summed = functools.reduce(jnp.add, weights)
        summed = jnp.broadcast_to(jnp.sum(summed, axis=1, keepdims=True), summed.shape)
        mixed = None
        for where, factors in parts:
            now, weights = weights[: len(factors)], weights[len(factors) :]
            now = jnp.concatenate([w.astype(jnp.bfloat16) for w in now], axis=1)
            term = jnp.dot(now, vbuf[where, columns], preferred_element_type=jnp.float32)
            mixed = term if mixed is None else mixed + term
        return high * EXP_SCALE, summed, mixed

    def help_group(g):
        for j in range(GROUPS[g]):
            head = FIRST[g] + j
            columns = slice(head * HEAD_DIM, (head + 1) * HEAD_DIM)
            high, summed, mixed = attend(
                qy, head, ((near, (F_NEAR,)), (slice(OWN * rows, (ZP + 1) * rows), (F_OWN, F_ZPY)))
            )
            give_o[:, columns] = (mixed / summed).astype(give_o.dtype)
            size = high + jnp.log2(summed)
            give_l[g, j : j + 1] = jnp.sum(jnp.where(diagonal, size, 0.0), axis=0, keepdims=True)

    def local_group(g):
        for j in range(GROUPS[g]):
            head = FIRST[g] + j
            top[head], tot[head], acc[head] = attend(
                qv, head, ((slice(SIB * rows, (ZM + 1) * rows), (None, None, F_ZP, F_ZM)),)
            )

    def merge_group(g):
        for kind in (1, 2):
            to_y(kind, g).wait_recv()
        for j in range(GROUPS[g]):
            head = FIRST[g] + j
            columns = slice(head * HEAD_DIM, (head + 1) * HEAD_DIM)
            size = jnp.broadcast_to(take_l[g, j : j + 1], (rows, rows))
            size = jnp.sum(jnp.where(diagonal, size, 0.0), axis=1, keepdims=True)
            size = jnp.broadcast_to(size, (rows, rows))
            high = jnp.maximum(top[head], size)
            mine = jnp.exp2(top[head] - high)
            theirs = jnp.exp2(size - high)
            mixed = acc[head] * mine + take_o[:, columns].astype(jnp.float32) * theirs
            mixed_heads[:, columns] = (mixed / (tot[head] * mine + theirs)).astype(mixed_heads.dtype)

    for load in loads:
        load.wait()
    for kv in range(2):
        to_sib(kv).wait_recv()

    for g in range(count):

        @pl.when(has_p)
        def _():
            for kv in range(2):
                along_z(TO_ZM, g, kv).wait_recv()

        @pl.when(has_p & gives)
        def _():
            for kv in range(2):
                along_z(HAND, g, kv).start()

        to_y(0, g).wait_recv()

        @pl.when(has_p & takes)
        def _():
            for kv in range(2):
                along_z(HAND, g, kv).wait_recv()

        help_group(g)
        for kind in (1, 2):
            to_y(kind, g).start()

        @pl.when(has_m)
        def _():
            for kv in range(2):
                along_z(TO_ZP, g, kv).wait_recv()

        local_group(g)
        if g >= LAG:
            merge_group(g - LAG)

    load_w.wait()
    for g in range(count - LAG, count - 1):
        merge_group(g)
    early = FIRST[-1] * HEAD_DIM
    projected = jnp.dot(mixed_heads[:, :early], wv[:early], preferred_element_type=jnp.float32)
    picks_to_y.wait_send()
    for kv in range(2):
        to_sib(kv).wait_send()
    for g in range(count):
        for kind in range(3 if g < count - 1 else 1):
            to_y(kind, g).wait_send()

    @pl.when(has_p)
    def _():
        for g in range(count):
            for kv in range(2):
                along_z(TO_ZP, g, kv).wait_send()

    @pl.when(has_m)
    def _():
        for g in range(count):
            for kv in range(2):
                along_z(TO_ZM, g, kv).wait_send()

    @pl.when(has_p & gives)
    def _():
        for g in range(count):
            for kv in range(2):
                along_z(HAND, g, kv).wait_send()

    merge_group(count - 1)
    projected = projected + jnp.dot(mixed_heads[:, early:], wv[early:], preferred_element_type=jnp.float32)
    out[...] = projected.astype(out.dtype)
    for kind in (1, 2):
        to_y(kind, count - 1).wait_send()


def attention(devices, queries, keys, values, far_picks, out_weight):
    rows, width = queries.shape
    count = len(GROUPS)
    in_hbm = pl.BlockSpec(memory_space=pltpu.HBM)
    per_head = pltpu.VMEM((HEADS, rows, HEAD_DIM), jnp.float32)
    wide = pltpu.VMEM((rows, width), jnp.bfloat16)
    sizes = pltpu.VMEM((count, 8, rows), jnp.float32)
    dma = pltpu.SemaphoreType.DMA
    return pl.pallas_call(
        functools.partial(kernel, devices),
        out_shape=jax.ShapeDtypeStruct((rows, width), jnp.bfloat16),
        in_specs=[in_hbm] * 5,
        out_specs=pl.BlockSpec(memory_space=pltpu.VMEM),
        scratch_shapes=[
            pltpu.SMEM(far_picks.shape, jnp.int32),
            pltpu.SMEM(far_picks.shape, jnp.int32),
            wide,
            wide,
            pltpu.VMEM(out_weight.shape, jnp.bfloat16),
            pltpu.VMEM((5 * rows, width), jnp.bfloat16),
            pltpu.VMEM((5 * rows, width), jnp.bfloat16),
            pltpu.VMEM((5, rows, rows), jnp.float32),
            per_head,
            per_head,
            per_head,
            wide,
            sizes,
            wide,
            sizes,
            wide,
            dma((5,)),
            dma((3, count, 2)),
            dma((3, count, 2)),
            dma((2,)),
            dma((2,)),
            dma((3, count)),
            dma((3, count)),
            dma,
            dma,
        ],
        compiler_params=pltpu.CompilerParams(
            collective_id=0, has_side_effects=True, vmem_limit_bytes=56_000_000
        ),
        name="helper_attention",
    )(*(pltpu.with_memory_space_constraint(x, pltpu.HBM) for x in (far_picks, queries, keys, values, out_weight)))


def solution(mesh):
    devices = mesh.shape["tm"]

    def body(queries, keys, values, far_picks, out_weight):
        return attention(devices, queries, keys, values, far_picks, out_weight)

    placed = (
        P(("vid", "tm"), None),
        P(("vid", "tm"), None),
        P(("vid", "tm"), None),
        P(("vid", "tm"), None),
        P(),
    )
    return jax.shard_map(
        body, mesh=mesh, in_specs=placed, out_specs=P(("vid", "tm"), None), check_vma=False
    )
```

```python
import functools
import math

import jax
import jax.numpy as jnp
from jax import lax
from jax.experimental import pallas as pl
from jax.experimental.pallas import tpu as pltpu
from jax.sharding import PartitionSpec as P

HEADS = 12
HEAD_DIM = 128
BLK = 64
NEG = -1e30
EXP_SCALE = HEAD_DIM ** (-0.5) * math.log2(math.e)
XF, SIB, OWN, ZP, ZM = range(5)
TO_ZP, TO_ZM, HAND = range(3)
YN, DG, XR = range(3)
R_Y, R_Z, R_SIB = range(3)
F_ZP, F_ZM, F_OWN, F_ZPY, F_NEAR, F_YN, F_DG, F_XR = range(8)
MESH = pl.DeviceIdType.MESH
GROUPS = (4, 3, 2, 2)
RELAYED = 1
SPANS = GROUPS + (RELAYED,)
FIRST = tuple(sum(SPANS[:g]) for g in range(len(SPANS)))
HELD = 4
EARLY = 1


def kernel(
    devices,
    picks_hbm,
    q_hbm,
    k_hbm,
    v_hbm,
    w_hbm,
    out,
    picks,
    picks_y,
    qv,
    qy,
    wv,
    kbuf,
    vbuf,
    krel,
    vrel,
    mult,
    top,
    tot,
    acc,
    give_o,
    give_l,
    take_o,
    take_l,
    mixed_heads,
    projected,
    load_sem,
    send_z,
    recv_z,
    send_sib,
    recv_sib,
    send_y,
    recv_y,
    send_p,
    recv_p,
    send_r,
    recv_r,
):
    rows = q_hbm.shape[0]
    chips = devices // 2
    count = len(GROUPS)
    p = lax.axis_index("tm")
    chip = p // 2
    core = p % 2
    even = chip % 2 == 0
    step = jnp.where(even, 1, -1)
    has_p = (chip + 2 * step >= 0) & (chip + 2 * step < chips)
    has_m = (chip - 2 * step >= 0) & (chip - 2 * step < chips)
    gives = (core + chip) % 2 == 0
    takes = jnp.logical_not(gives)

    sib = p + 1 - 2 * core
    y_dev = p + 2 * step
    zp_dev = p + 4 * step
    zm_dev = p - 4 * step
    bufs = (kbuf, vbuf)
    hbms = (k_hbm, v_hbm)
    rels = (krel, vrel)

    def columns_of(g):
        return pl.ds(FIRST[g] * HEAD_DIM, SPANS[g] * HEAD_DIM)

    def slot(index):
        return pl.ds(index * rows, rows)

    def remote(src, dst, send, recv, dev):
        return pltpu.make_async_remote_copy(
            src_ref=src, dst_ref=dst, send_sem=send, recv_sem=recv, device_id={"tm": dev}, device_id_type=MESH
        )

    def along_z(kind, g, kv):
        dst, dev = ((ZM, zp_dev), (ZP, zm_dev), (XF, sib))[kind]
        columns = columns_of(g)
        src = bufs[kv].at[slot(ZP), columns] if kind == HAND else hbms[kv].at[:, columns]
        where = (kind, g, kv)
        return remote(src, bufs[kv].at[slot(dst), columns], send_z.at[where], recv_z.at[where], dev)

    def to_sib(kv):
        return remote(hbms[kv], bufs[kv].at[slot(SIB)], send_sib.at[kv], recv_sib.at[kv], sib)

    def to_y(kind, g):
        columns = columns_of(g)
        src, dst = (
            (q_hbm.at[:, columns], qy.at[:, columns]),
            (give_o.at[:, columns], take_o.at[:, columns]),
            (give_l.at[g], take_l.at[g]),
        )[kind]
        return remote(src, dst, send_y.at[kind, g], recv_y.at[kind, g], y_dev)

    def relayed(kind, kv, given=YN):
        src = hbms[kv].at[:, columns_of(count)] if kind == R_Y else rels[kv].at[slot(given)]
        dst, dev = ((YN, y_dev), (DG, zp_dev), (XR, sib))[kind]
        return remote(src, rels[kv].at[slot(dst)], send_r.at[kind, kv], recv_r.at[kind, kv], dev)

    picks_to_y = remote(picks_hbm, picks_y, send_p, recv_p, y_dev)
    load_w = pltpu.make_async_copy(w_hbm, wv, load_sem.at[4])
    load_picks = pltpu.make_async_copy(picks_hbm, picks, load_sem.at[3])
    load_picks.start()
    loads = [
        pltpu.make_async_copy(q_hbm, qv, load_sem.at[0]),
        pltpu.make_async_copy(k_hbm, kbuf.at[slot(OWN)], load_sem.at[1]),
        pltpu.make_async_copy(v_hbm, vbuf.at[slot(OWN)], load_sem.at[2]),
    ]
    for load in loads:
        load.start()

    barrier = pltpu.get_barrier_semaphore()

    def greet(dev):
        pl.semaphore_signal(barrier, inc=1, device_id={"tm": dev}, device_id_type=MESH)

    greet(sib)
    greet(y_dev)

    @pl.when(has_p)
    def _():
        greet(zp_dev)

    @pl.when(has_m)
    def _():
        greet(zm_dev)

    pl.semaphore_wait(barrier, 2 + jnp.where(has_p, 1, 0) + jnp.where(has_m, 1, 0))

    def send_zm(g):
        @pl.when(has_m)
        def _():
            for kv in range(2):
                along_z(TO_ZM, g, kv).start()

    def send_zp(g):
        @pl.when(has_p)
        def _():
            for kv in range(2):
                along_z(TO_ZP, g, kv).start()

    send_zm(0)
    for kv in range(2):
        relayed(R_Y, kv).start()
    send_zp(0)
    picks_to_y.start()
    to_y(0, 0).start()
    for kv in range(2):
        to_sib(kv).start()
    for g in range(1, count + 1):
        send_zm(g)
        if g < HELD:
            send_zp(g)
        if g < count:
            to_y(0, g).start()

    load_w.start()
    load_picks.wait()
    picks_to_y.wait_recv()

    ints = jnp.int32
    row_at = lax.broadcasted_iota(ints, (rows, rows), 0)
    col_at = lax.broadcasted_iota(ints, (rows, rows), 1)
    row_first = row_at < BLK
    col_first = col_at < BLK
    diagonal = row_at == col_at

    def fill(index, named, up, down, valid):
        one = jnp.where(valid, 1, 0)
        seconds = [
            jnp.where(even, named[b, up] + named[b, up + 1], named[b, down] + named[b, down + 1]) for b in range(2)
        ]
        cells = [[((2 - n) * one).astype(jnp.float32), (n * one).astype(jnp.float32)] for n in seconds]
        mult[index] = jnp.where(
            row_first,
            jnp.where(col_first, cells[0][0], cells[0][1]),
            jnp.where(col_first, cells[1][0], cells[1][1]),
        )

    near_valid = gives | has_p
    fill(F_ZP, picks, 6, 2, has_p)
    fill(F_ZM, picks, 2, 6, has_m)
    fill(F_OWN, picks_y, 0, 4, True)
    fill(F_ZPY, picks_y, 4, 0, has_p)
    fill(F_YN, picks, 4, 0, True)
    fill(F_DG, picks, 0, 4, has_m)
    over_valid = takes | has_m
    mult[F_XR] = jnp.full((rows, rows), jnp.where(over_valid, 1.0, 0.0), jnp.float32)
    mult[F_NEAR] = jnp.full((rows, rows), jnp.where(near_valid, 1.0, 0.0), jnp.float32)

    def clear(ref, index):
        ref[index * rows : (index + 1) * rows] = jnp.zeros((rows, ref.shape[1]), ref.dtype)

    @pl.when(jnp.logical_not(has_p))
    def _():
        clear(vbuf, ZP)

    @pl.when(jnp.logical_not(has_m))
    def _():
        clear(vbuf, ZM)
        clear(vrel, DG)

    @pl.when(jnp.logical_not(near_valid))
    def _():
        clear(vbuf, XF)

    @pl.when(jnp.logical_not(over_valid))
    def _():
        clear(vrel, XR)

    near = pl.ds(pl.multiple_of(jnp.where(gives, SIB, XF) * rows, rows), rows)

    def weigh(query, head, parts):
        columns = slice(head * HEAD_DIM, (head + 1) * HEAD_DIM)
        pieces = []
        for k_from, _, factors in parts:
            scores = lax.dot_general(
                query[:, columns],
                k_from[...],
                (((1,), (1,)), ((), ())),
                preferred_element_type=jnp.float32,
            )
            for i, factor in enumerate(factors):
                piece = scores[:, i * rows : (i + 1) * rows]
                if factor is not None:
                    piece = jnp.where(mult[factor] > 0, piece, NEG)
                pieces.append((piece, factor))
        high = functools.reduce(jnp.maximum, [piece for piece, _ in pieces])
        high = jnp.broadcast_to(jnp.max(high, axis=1, keepdims=True), high.shape)
        weights = []
        for piece, factor in pieces:
            weight = jnp.exp2((piece - high) * EXP_SCALE)
            if factor is not None:
                weight = weight * mult[factor]
            weights.append(weight)
        summed = functools.reduce(jnp.add, weights)
        summed = jnp.broadcast_to(jnp.sum(summed, axis=1, keepdims=True), summed.shape)
        return high * EXP_SCALE, summed, [weight.astype(jnp.bfloat16) for weight in weights]

    def gather(weights, parts):
        mixed = None
        for _, v_from, factors in parts:
            now, weights = weights[: len(factors)], weights[len(factors) :]
            now = jnp.concatenate(now, axis=1)
            term = jnp.dot(now, v_from[...], preferred_element_type=jnp.float32)
            mixed = term if mixed is None else mixed + term
        return mixed

    def held(where, head, factors):
        columns = pl.ds(head * HEAD_DIM, HEAD_DIM)
        return kbuf.at[where, columns], vbuf.at[where, columns], factors

    def help_parts(head):
        return held(near, head, (F_NEAR,)), held(pl.ds(OWN * rows, 2 * rows), head, (F_OWN, F_ZPY))

    def heads_of(g):
        return range(FIRST[g], FIRST[g] + SPANS[g])

    def help_weigh(g):
        found = [weigh(qy, head, help_parts(head)) for head in heads_of(g)]
        for j, (high, summed, _) in enumerate(found):
            size = high + jnp.log2(summed)
            give_l[g, j : j + 1] = jnp.sum(jnp.where(diagonal, size, 0.0), axis=0, keepdims=True)
        return found

    def help_gather(g, found):
        for head, (_, summed, weights) in zip(heads_of(g), found):
            columns = slice(head * HEAD_DIM, (head + 1) * HEAD_DIM)
            mixed = gather(weights, help_parts(head))
            give_o[:, columns] = (mixed / summed).astype(give_o.dtype)

    def near_part(head):
        return held(pl.ds(SIB * rows, 4 * rows), head, (None, None, F_ZP, F_ZM))

    def local_weigh(g):
        found = [weigh(qv, head, (near_part(head),)) for head in heads_of(g)]
        for head, (high, summed, _) in zip(heads_of(g), found):
            top[head], tot[head] = high, summed
        return [weights for _, _, weights in found]

    def local_gather(g, found):
        for head, weights in zip(heads_of(g), found):
            acc[head] = gather(weights, (near_part(head),))

    def relayed_parts(head):
        mine = pl.ds((head - FIRST[count]) * HEAD_DIM, HEAD_DIM)
        return near_part(head), (krel.at[:, mine], vrel.at[:, mine], (F_YN, F_DG, F_XR))

    def relayed_ready(kv):
        @pl.when(has_p)
        def _():
            along_z(TO_ZM, count, kv).wait_recv()

        below_ready(count, kv)

        @pl.when(over_valid)
        def _():
            relayed(R_SIB, kv).wait_recv()

    def relayed_weigh():
        return [weigh(qv, head, relayed_parts(head)) for head in heads_of(count)]

    def relayed_gather(found):
        for head, (_, summed, weights) in zip(heads_of(count), found):
            columns = slice(head * HEAD_DIM, (head + 1) * HEAD_DIM)
            mixed = gather(weights, relayed_parts(head))
            mixed_heads[:, columns] = (mixed / summed).astype(mixed_heads.dtype)

    def merge_group(g):
        for kind in (1, 2):
            to_y(kind, g).wait_recv()
        for j in range(GROUPS[g]):
            head = FIRST[g] + j
            columns = slice(head * HEAD_DIM, (head + 1) * HEAD_DIM)
            size = jnp.broadcast_to(take_l[g, j : j + 1], (rows, rows))
            size = jnp.sum(jnp.where(diagonal, size, 0.0), axis=1, keepdims=True)
            size = jnp.broadcast_to(size, (rows, rows))
            high = jnp.maximum(top[head], size)
            mine = jnp.exp2(top[head] - high)
            theirs = jnp.exp2(size - high)
            mixed = acc[head] * mine + take_o[:, columns].astype(jnp.float32) * theirs
            mixed_heads[:, columns] = (mixed / (tot[head] * mine + theirs)).astype(mixed_heads.dtype)

    for load in loads:
        load.wait()
    for kv in range(2):
        to_sib(kv).wait_recv()
    def relay():
        for kv in range(2):
            relayed(R_Y, kv).wait_recv()

        @pl.when(has_p)
        def _():
            for kv in range(2):
                relayed(R_Z, kv).start()

        for g in range(HELD, count + 1):
            send_zp(g)

        @pl.when(gives)
        def _():
            for kv in range(2):
                relayed(R_SIB, kv).start()

    def above_ready(g, kv):
        @pl.when(has_p)
        def _():
            along_z(TO_ZM, g, kv).wait_recv()

        @pl.when(has_p & gives)
        def _():
            along_z(HAND, g, kv).start()

    def handed(g, kv):
        @pl.when(has_p & takes)
        def _():
            along_z(HAND, g, kv).wait_recv()

    def below_ready(g, kv):
        @pl.when(has_m)
        def _():
            along_z(TO_ZP, g, kv).wait_recv()

    def project(first, end):
        rows_of = slice(FIRST[first] * HEAD_DIM, (FIRST[end - 1] + SPANS[end - 1]) * HEAD_DIM)
        return jnp.dot(mixed_heads[:, rows_of], wv[rows_of], preferred_element_type=jnp.float32)

    for g in range(count):
        if g == count - 1:
            load_w.wait()
            for done in range(EARLY):
                merge_group(done)
            projected[...] = project(0, EARLY)
        if g > 0:
            below_ready(g - 1, 1)
            local_gather(g - 1, nearby)
        above_ready(g, 0)
        to_y(0, g).wait_recv()
        handed(g, 0)
        found = help_weigh(g)
        above_ready(g, 1)
        below_ready(g, 0)
        nearby = local_weigh(g)
        handed(g, 1)
        help_gather(g, found)
        for kind in (1, 2):
            to_y(kind, g).start()
        if g == 1:
            relay()

    @pl.when(has_m)
    def _():
        for kv in range(2):
            relayed(R_Z, kv).wait_recv()

    @pl.when(has_m & takes)
    def _():
        for kv in range(2):
            relayed(R_SIB, kv, DG).start()

    below_ready(count - 1, 1)
    local_gather(count - 1, nearby)
    for g in range(EARLY, count - 1):
        merge_group(g)
    projected[...] += project(EARLY, count - 1)
    relayed_ready(0)
    found = relayed_weigh()
    relayed_ready(1)

    def sends_done(first, end):
        for kind, sent in ((TO_ZP, has_p), (TO_ZM, has_m)):

            @pl.when(sent)
            def _():
                for g in range(first, end):
                    for kv in range(2):
                        along_z(kind, g, kv).wait_send()

    relayed_gather(found)
    picks_to_y.wait_send()
    for kv in range(2):
        to_sib(kv).wait_send()
        relayed(R_Y, kv).wait_send()
    for g in range(count):
        for kind in range(3 if g < count - 1 else 1):
            to_y(kind, g).wait_send()

    @pl.when(has_p & gives)
    def _():
        for g in range(count - 1):
            for kv in range(2):
                along_z(HAND, g, kv).wait_send()

    sends_done(0, 1)

    merge_group(count - 1)
    out[...] = (projected[...] + project(count - 1, count + 1)).astype(out.dtype)
    for kind in (1, 2):
        to_y(kind, count - 1).wait_send()
    sends_done(1, count + 1)

    @pl.when(has_p)
    def _():
        for kv in range(2):
            relayed(R_Z, kv).wait_send()

    @pl.when(gives | has_m)
    def _():
        for kv in range(2):
            relayed(R_SIB, kv).wait_send()

    @pl.when(has_p & gives)
    def _():
        for kv in range(2):
            along_z(HAND, count - 1, kv).wait_send()


def attention(devices, queries, keys, values, far_picks, out_weight):
    rows, width = queries.shape
    count = len(GROUPS)
    in_hbm = pl.BlockSpec(memory_space=pltpu.HBM)
    per_head = pltpu.VMEM((HEADS, rows, HEAD_DIM), jnp.float32)
    wide = pltpu.VMEM((rows, width), jnp.bfloat16)
    sizes = pltpu.VMEM((count, 8, rows), jnp.float32)
    over = pltpu.VMEM((3 * rows, RELAYED * HEAD_DIM), jnp.bfloat16)
    dma = pltpu.SemaphoreType.DMA
    return pl.pallas_call(
        functools.partial(kernel, devices),
        out_shape=jax.ShapeDtypeStruct((rows, width), jnp.bfloat16),
        in_specs=[in_hbm] * 5,
        out_specs=pl.BlockSpec(memory_space=pltpu.VMEM),
        scratch_shapes=[
            pltpu.SMEM(far_picks.shape, jnp.int32),
            pltpu.SMEM(far_picks.shape, jnp.int32),
            wide,
            wide,
            pltpu.VMEM(out_weight.shape, jnp.bfloat16),
            pltpu.VMEM((5 * rows, width), jnp.bfloat16),
            pltpu.VMEM((5 * rows, width), jnp.bfloat16),
            over,
            over,
            pltpu.VMEM((8, rows, rows), jnp.float32),
            per_head,
            per_head,
            per_head,
            wide,
            sizes,
            wide,
            sizes,
            wide,
            pltpu.VMEM((rows, width), jnp.float32),
            dma((5,)),
            dma((3, count + 1, 2)),
            dma((3, count + 1, 2)),
            dma((2,)),
            dma((2,)),
            dma((3, count)),
            dma((3, count)),
            dma,
            dma,
            dma((3, 2)),
            dma((3, 2)),
        ],
        compiler_params=pltpu.CompilerParams(
            collective_id=0, has_side_effects=True, vmem_limit_bytes=56_000_000
        ),
        name="helper_attention",
    )(*(pltpu.with_memory_space_constraint(x, pltpu.HBM) for x in (far_picks, queries, keys, values, out_weight)))


def solution(mesh):
    devices = mesh.shape["tm"]

    def body(queries, keys, values, far_picks, out_weight):
        return attention(devices, queries, keys, values, far_picks, out_weight)

    placed = (
        P(("vid", "tm"), None),
        P(("vid", "tm"), None),
        P(("vid", "tm"), None),
        P(("vid", "tm"), None),
        P(),
    )
    return jax.shard_map(
        body, mesh=mesh, in_specs=placed, out_specs=P(("vid", "tm"), None), check_vma=False
    )
```

```python
import functools
import math

import jax
import jax.numpy as jnp
from jax import lax
from jax.experimental import pallas as pl
from jax.experimental.pallas import tpu as pltpu
from jax.sharding import PartitionSpec as P

HEADS = 12
HEAD_DIM = 128
BLK = 64
NEG = -1e30
EXP_SCALE = HEAD_DIM ** (-0.5) * math.log2(math.e)
XF, SIB, OWN, ZP, ZM = range(5)
TO_ZP, TO_ZM, HAND = range(3)
YN, DG, XR = range(3)
R_Y, R_Z, R_SIB = range(3)
F_ZP, F_ZM, F_OWN, F_ZPY, F_NEAR, F_YN, F_DG, F_XR = range(8)
MESH = pl.DeviceIdType.MESH
GROUPS = (4, 3, 2, 2)
RELAYED = 1
SPANS = GROUPS + (RELAYED,)
FIRST = tuple(sum(SPANS[:g]) for g in range(len(SPANS)))
HELD = 4
EARLY = 1


def kernel(
    devices,
    picks_hbm,
    q_hbm,
    k_hbm,
    v_hbm,
    w_hbm,
    out,
    picks,
    picks_y,
    qv,
    qy,
    wv,
    kbuf,
    vbuf,
    krel,
    vrel,
    mult,
    top,
    tot,
    acc,
    give_o,
    give_l,
    take_o,
    take_l,
    mixed_heads,
    projected,
    kept,
    kept_sum,
    load_sem,
    send_z,
    recv_z,
    send_sib,
    recv_sib,
    send_y,
    recv_y,
    send_p,
    recv_p,
    send_r,
    recv_r,
):
    rows = q_hbm.shape[0]
    chips = devices // 2
    count = len(GROUPS)
    p = lax.axis_index("tm")
    chip = p // 2
    core = p % 2
    even = chip % 2 == 0
    step = jnp.where(even, 1, -1)
    has_p = (chip + 2 * step >= 0) & (chip + 2 * step < chips)
    has_m = (chip - 2 * step >= 0) & (chip - 2 * step < chips)
    gives = (core + chip) % 2 == 0
    takes = jnp.logical_not(gives)

    sib = p + 1 - 2 * core
    y_dev = p + 2 * step
    zp_dev = p + 4 * step
    zm_dev = p - 4 * step
    bufs = (kbuf, vbuf)
    hbms = (k_hbm, v_hbm)
    rels = (krel, vrel)

    def columns_of(g):
        return pl.ds(FIRST[g] * HEAD_DIM, SPANS[g] * HEAD_DIM)

    def slot(index):
        return pl.ds(index * rows, rows)

    def remote(src, dst, send, recv, dev):
        return pltpu.make_async_remote_copy(
            src_ref=src, dst_ref=dst, send_sem=send, recv_sem=recv, device_id={"tm": dev}, device_id_type=MESH
        )

    def along_z(kind, g, kv):
        dst, dev = ((ZM, zp_dev), (ZP, zm_dev), (XF, sib))[kind]
        columns = columns_of(g)
        src = bufs[kv].at[slot(ZP), columns] if kind == HAND else hbms[kv].at[:, columns]
        where = (kind, g, kv)
        return remote(src, bufs[kv].at[slot(dst), columns], send_z.at[where], recv_z.at[where], dev)

    def to_sib(kv):
        return remote(hbms[kv], bufs[kv].at[slot(SIB)], send_sib.at[kv], recv_sib.at[kv], sib)

    def to_y(kind, g):
        columns = columns_of(g)
        src, dst = (
            (q_hbm.at[:, columns], qy.at[:, columns]),
            (give_o.at[:, columns], take_o.at[:, columns]),
            (give_l.at[g], take_l.at[g]),
        )[kind]
        return remote(src, dst, send_y.at[kind, g], recv_y.at[kind, g], y_dev)

    def relayed(kind, kv, given=YN):
        src = hbms[kv].at[:, columns_of(count)] if kind == R_Y else rels[kv].at[slot(given)]
        dst, dev = ((YN, y_dev), (DG, zp_dev), (XR, sib))[kind]
        return remote(src, rels[kv].at[slot(dst)], send_r.at[kind, kv], recv_r.at[kind, kv], dev)

    picks_to_y = remote(picks_hbm, picks_y, send_p, recv_p, y_dev)
    load_w = pltpu.make_async_copy(w_hbm, wv, load_sem.at[4])
    load_picks = pltpu.make_async_copy(picks_hbm, picks, load_sem.at[3])
    load_picks.start()
    loads = [
        pltpu.make_async_copy(q_hbm, qv, load_sem.at[0]),
        pltpu.make_async_copy(k_hbm, kbuf.at[slot(OWN)], load_sem.at[1]),
        pltpu.make_async_copy(v_hbm, vbuf.at[slot(OWN)], load_sem.at[2]),
    ]
    for load in loads:
        load.start()

    barrier = pltpu.get_barrier_semaphore()

    def greet(dev):
        pl.semaphore_signal(barrier, inc=1, device_id={"tm": dev}, device_id_type=MESH)

    greet(sib)
    greet(y_dev)

    @pl.when(has_p)
    def _():
        greet(zp_dev)

    @pl.when(has_m)
    def _():
        greet(zm_dev)

    pl.semaphore_wait(barrier, 2 + jnp.where(has_p, 1, 0) + jnp.where(has_m, 1, 0))

    def send_zm(g):
        @pl.when(has_m)
        def _():
            for kv in range(2):
                along_z(TO_ZM, g, kv).start()

    def send_zp(g):
        @pl.when(has_p)
        def _():
            for kv in range(2):
                along_z(TO_ZP, g, kv).start()

    send_zm(0)
    for kv in range(2):
        relayed(R_Y, kv).start()
    send_zp(0)
    picks_to_y.start()
    to_y(0, 0).start()
    for kv in range(2):
        to_sib(kv).start()
    for g in range(1, count + 1):
        send_zm(g)
        if g < HELD:
            send_zp(g)
        if g < count:
            to_y(0, g).start()

    load_w.start()
    load_picks.wait()
    picks_to_y.wait_recv()

    ints = jnp.int32
    row_at = lax.broadcasted_iota(ints, (rows, rows), 0)
    col_at = lax.broadcasted_iota(ints, (rows, rows), 1)
    row_first = row_at < BLK
    col_first = col_at < BLK
    diagonal = row_at == col_at

    def fill(index, named, up, down, valid):
        one = jnp.where(valid, 1, 0)
        seconds = [
            jnp.where(even, named[b, up] + named[b, up + 1], named[b, down] + named[b, down + 1]) for b in range(2)
        ]
        cells = [[((2 - n) * one).astype(jnp.float32), (n * one).astype(jnp.float32)] for n in seconds]
        mult[index] = jnp.where(
            row_first,
            jnp.where(col_first, cells[0][0], cells[0][1]),
            jnp.where(col_first, cells[1][0], cells[1][1]),
        )

    near_valid = gives | has_p
    fill(F_ZP, picks, 6, 2, has_p)
    fill(F_ZM, picks, 2, 6, has_m)
    fill(F_OWN, picks_y, 0, 4, True)
    fill(F_ZPY, picks_y, 4, 0, has_p)
    fill(F_YN, picks, 4, 0, True)
    fill(F_DG, picks, 0, 4, has_m)
    over_valid = takes | has_m
    mult[F_XR] = jnp.full((rows, rows), jnp.where(over_valid, 1.0, 0.0), jnp.float32)
    mult[F_NEAR] = jnp.full((rows, rows), jnp.where(near_valid, 1.0, 0.0), jnp.float32)

    def clear(ref, index):
        ref[index * rows : (index + 1) * rows] = jnp.zeros((rows, ref.shape[1]), ref.dtype)

    @pl.when(jnp.logical_not(has_p))
    def _():
        clear(vbuf, ZP)

    @pl.when(jnp.logical_not(has_m))
    def _():
        clear(vbuf, ZM)
        clear(vrel, DG)

    @pl.when(jnp.logical_not(near_valid))
    def _():
        clear(vbuf, XF)

    @pl.when(jnp.logical_not(over_valid))
    def _():
        clear(vrel, XR)

    near = pl.ds(pl.multiple_of(jnp.where(gives, SIB, XF) * rows, rows), rows)

    def weigh(query, head, parts):
        columns = slice(head * HEAD_DIM, (head + 1) * HEAD_DIM)
        pieces = []
        for k_from, _, factors in parts:
            scores = lax.dot_general(
                query[:, columns],
                k_from[...],
                (((1,), (1,)), ((), ())),
                preferred_element_type=jnp.float32,
            )
            for i, factor in enumerate(factors):
                piece = scores[:, i * rows : (i + 1) * rows]
                if factor is not None:
                    piece = jnp.where(mult[factor] > 0, piece, NEG)
                pieces.append((piece, factor))
        high = functools.reduce(jnp.maximum, [piece for piece, _ in pieces])
        high = jnp.broadcast_to(jnp.max(high, axis=1, keepdims=True), high.shape)
        weights = []
        for piece, factor in pieces:
            weight = jnp.exp2((piece - high) * EXP_SCALE)
            if factor is not None:
                weight = weight * mult[factor]
            weights.append(weight)
        summed = functools.reduce(jnp.add, weights)
        summed = jnp.broadcast_to(jnp.sum(summed, axis=1, keepdims=True), summed.shape)
        return high * EXP_SCALE, summed, [weight.astype(jnp.bfloat16) for weight in weights]

    def gather(weights, parts):
        mixed = None
        for _, v_from, factors in parts:
            now, weights = weights[: len(factors)], weights[len(factors) :]
            now = jnp.concatenate(now, axis=1)
            term = jnp.dot(now, v_from[...], preferred_element_type=jnp.float32)
            mixed = term if mixed is None else mixed + term
        return mixed

    def held(where, head, factors):
        columns = pl.ds(head * HEAD_DIM, HEAD_DIM)
        return kbuf.at[where, columns], vbuf.at[where, columns], factors

    def help_parts(head):
        return held(near, head, (F_NEAR,)), held(pl.ds(OWN * rows, 2 * rows), head, (F_OWN, F_ZPY))

    def heads_of(g):
        return range(FIRST[g], FIRST[g] + SPANS[g])

    def help_weigh(g):
        found = [weigh(qy, head, help_parts(head)) for head in heads_of(g)]
        for j, (high, summed, _) in enumerate(found):
            size = high + jnp.log2(summed)
            give_l[g, j : j + 1] = jnp.sum(jnp.where(diagonal, size, 0.0), axis=0, keepdims=True)
        return found

    def help_gather(g, found):
        for head, (_, summed, weights) in zip(heads_of(g), found):
            columns = slice(head * HEAD_DIM, (head + 1) * HEAD_DIM)
            mixed = gather(weights, help_parts(head))
            give_o[:, columns] = (mixed / summed).astype(give_o.dtype)

    def near_part(head):
        return held(pl.ds(SIB * rows, 4 * rows), head, (None, None, F_ZP, F_ZM))

    def local_weigh(g):
        found = [weigh(qv, head, (near_part(head),)) for head in heads_of(g)]
        for head, (high, summed, _) in zip(heads_of(g), found):
            top[head], tot[head] = high, summed
        return [weights for _, _, weights in found]

    def local_gather(g, found):
        for head, weights in zip(heads_of(g), found):
            acc[head] = gather(weights, (near_part(head),))

    def relayed_parts(head):
        mine = pl.ds((head - FIRST[count]) * HEAD_DIM, HEAD_DIM)
        return near_part(head), (krel.at[:, mine], vrel.at[:, mine], (F_YN, F_DG, F_XR))

    def relayed_ready(kv):
        @pl.when(has_p)
        def _():
            along_z(TO_ZM, count, kv).wait_recv()

        below_ready(count, kv)

        @pl.when(over_valid)
        def _():
            relayed(R_SIB, kv).wait_recv()

    def relayed_weigh():
        return [weigh(qv, head, relayed_parts(head)) for head in heads_of(count)]

    def relayed_gather(found):
        for head, (_, summed, weights) in zip(heads_of(count), found):
            columns = slice(head * HEAD_DIM, (head + 1) * HEAD_DIM)
            mixed = gather(weights, relayed_parts(head))
            mixed_heads[:, columns] = (mixed / summed).astype(mixed_heads.dtype)

    def merge_group(g):
        for kind in (1, 2):
            to_y(kind, g).wait_recv()
        for j in range(GROUPS[g]):
            head = FIRST[g] + j
            columns = slice(head * HEAD_DIM, (head + 1) * HEAD_DIM)
            size = jnp.broadcast_to(take_l[g, j : j + 1], (rows, rows))
            size = jnp.sum(jnp.where(diagonal, size, 0.0), axis=1, keepdims=True)
            size = jnp.broadcast_to(size, (rows, rows))
            high = jnp.maximum(top[head], size)
            mine = jnp.exp2(top[head] - high)
            theirs = jnp.exp2(size - high)
            mixed = acc[head] * mine + take_o[:, columns].astype(jnp.float32) * theirs
            mixed_heads[:, columns] = (mixed / (tot[head] * mine + theirs)).astype(mixed_heads.dtype)

    for load in loads:
        load.wait()
    for kv in range(2):
        to_sib(kv).wait_recv()
    def relay():
        for kv in range(2):
            relayed(R_Y, kv).wait_recv()

        @pl.when(has_p)
        def _():
            for kv in range(2):
                relayed(R_Z, kv).start()

        for g in range(HELD, count + 1):
            send_zp(g)

        @pl.when(gives)
        def _():
            for kv in range(2):
                relayed(R_SIB, kv).start()

    def above_ready(g, kv):
        @pl.when(has_p)
        def _():
            along_z(TO_ZM, g, kv).wait_recv()

        @pl.when(has_p & gives)
        def _():
            along_z(HAND, g, kv).start()

    def handed(g, kv):
        @pl.when(has_p & takes)
        def _():
            along_z(HAND, g, kv).wait_recv()

    def below_ready(g, kv):
        @pl.when(has_m)
        def _():
            along_z(TO_ZP, g, kv).wait_recv()

    def project(first, end):
        rows_of = slice(FIRST[first] * HEAD_DIM, (FIRST[end - 1] + SPANS[end - 1]) * HEAD_DIM)
        return jnp.dot(mixed_heads[:, rows_of], wv[rows_of], preferred_element_type=jnp.float32)

    def give(g):
        for kind in (1, 2):
            to_y(kind, g).start()

    final = count - 1
    for g in range(count):
        if g == final:
            load_w.wait()
            for done in range(EARLY):
                merge_group(done)
            projected[...] = project(0, EARLY)
        if g > 0:
            below_ready(g - 1, 1)
            local_gather(g - 1, nearby)
        above_ready(g, 0)
        handed(g, 0)
        if g < final:
            to_y(0, g).wait_recv()
            found = help_weigh(g)
        else:

            @pl.when(has_p)
            def _():
                to_y(0, final).wait_recv()
                for j, (_, summed, weights) in enumerate(help_weigh(final)):
                    kept_sum[j] = summed
                    for i, weight in enumerate(weights):
                        kept[j, i] = weight

        below_ready(g, 0)
        nearby = local_weigh(g)
        above_ready(g, 1)
        handed(g, 1)
        if g < final:
            help_gather(g, found)
            give(g)
        else:

            @pl.when(has_p)
            def _():
                help_gather(final, [(None, kept_sum[j], [kept[j, i] for i in range(3)]) for j in range(GROUPS[final])])
                give(final)

        if g == 1:
            relay()

            @pl.when(jnp.logical_not(has_p))
            def _():
                to_y(0, final).wait_recv()
                help_gather(final, help_weigh(final))
                give(final)

    @pl.when(has_m)
    def _():
        for kv in range(2):
            relayed(R_Z, kv).wait_recv()

    @pl.when(has_m & takes)
    def _():
        for kv in range(2):
            relayed(R_SIB, kv, DG).start()

    below_ready(count - 1, 1)
    local_gather(count - 1, nearby)
    for g in range(EARLY, count - 1):
        merge_group(g)
    projected[...] += project(EARLY, count - 1)
    relayed_ready(0)
    found = relayed_weigh()
    relayed_ready(1)

    def sends_done(first, end):
        for kind, sent in ((TO_ZP, has_p), (TO_ZM, has_m)):

            @pl.when(sent)
            def _():
                for g in range(first, end):
                    for kv in range(2):
                        along_z(kind, g, kv).wait_send()

    relayed_gather(found)
    picks_to_y.wait_send()
    for kv in range(2):
        to_sib(kv).wait_send()
        relayed(R_Y, kv).wait_send()
    for g in range(count):
        for kind in range(3 if g < count - 1 else 1):
            to_y(kind, g).wait_send()

    @pl.when(has_p & gives)
    def _():
        for g in range(count - 1):
            for kv in range(2):
                along_z(HAND, g, kv).wait_send()

    sends_done(0, 1)

    merge_group(count - 1)
    out[...] = (projected[...] + project(count - 1, count + 1)).astype(out.dtype)
    for kind in (1, 2):
        to_y(kind, count - 1).wait_send()
    sends_done(1, count + 1)

    @pl.when(has_p)
    def _():
        for kv in range(2):
            relayed(R_Z, kv).wait_send()

    @pl.when(gives | has_m)
    def _():
        for kv in range(2):
            relayed(R_SIB, kv).wait_send()

    @pl.when(has_p & gives)
    def _():
        for kv in range(2):
            along_z(HAND, count - 1, kv).wait_send()


def attention(devices, queries, keys, values, far_picks, out_weight):
    rows, width = queries.shape
    count = len(GROUPS)
    in_hbm = pl.BlockSpec(memory_space=pltpu.HBM)
    per_head = pltpu.VMEM((HEADS, rows, HEAD_DIM), jnp.float32)
    wide = pltpu.VMEM((rows, width), jnp.bfloat16)
    sizes = pltpu.VMEM((count, 8, rows), jnp.float32)
    over = pltpu.VMEM((3 * rows, RELAYED * HEAD_DIM), jnp.bfloat16)
    dma = pltpu.SemaphoreType.DMA
    return pl.pallas_call(
        functools.partial(kernel, devices),
        out_shape=jax.ShapeDtypeStruct((rows, width), jnp.bfloat16),
        in_specs=[in_hbm] * 5,
        out_specs=pl.BlockSpec(memory_space=pltpu.VMEM),
        scratch_shapes=[
            pltpu.SMEM(far_picks.shape, jnp.int32),
            pltpu.SMEM(far_picks.shape, jnp.int32),
            wide,
            wide,
            pltpu.VMEM(out_weight.shape, jnp.bfloat16),
            pltpu.VMEM((5 * rows, width), jnp.bfloat16),
            pltpu.VMEM((5 * rows, width), jnp.bfloat16),
            over,
            over,
            pltpu.VMEM((8, rows, rows), jnp.float32),
            per_head,
            per_head,
            per_head,
            wide,
            sizes,
            wide,
            sizes,
            wide,
            pltpu.VMEM((rows, width), jnp.float32),
            pltpu.VMEM((GROUPS[-1], 3, rows, rows), jnp.bfloat16),
            pltpu.VMEM((GROUPS[-1], rows, HEAD_DIM), jnp.float32),
            dma((5,)),
            dma((3, count + 1, 2)),
            dma((3, count + 1, 2)),
            dma((2,)),
            dma((2,)),
            dma((3, count)),
            dma((3, count)),
            dma,
            dma,
            dma((3, 2)),
            dma((3, 2)),
        ],
        compiler_params=pltpu.CompilerParams(
            collective_id=0, has_side_effects=True, vmem_limit_bytes=56_000_000
        ),
        name="helper_attention",
    )(*(pltpu.with_memory_space_constraint(x, pltpu.HBM) for x in (far_picks, queries, keys, values, out_weight)))


def solution(mesh):
    devices = mesh.shape["tm"]

    def body(queries, keys, values, far_picks, out_weight):
        return attention(devices, queries, keys, values, far_picks, out_weight)

    placed = (
        P(("vid", "tm"), None),
        P(("vid", "tm"), None),
        P(("vid", "tm"), None),
        P(("vid", "tm"), None),
        P(),
    )
    return jax.shard_map(
        body, mesh=mesh, in_specs=placed, out_specs=P(("vid", "tm"), None), check_vma=False
    )
```

```python
import functools
import math

import jax
import jax.numpy as jnp
from jax import lax
from jax.experimental import pallas as pl
from jax.experimental.pallas import tpu as pltpu
from jax.sharding import PartitionSpec as P

HEADS = 12
HEAD_DIM = 128
BLK = 64
NEG = -1e30
EXP_SCALE = HEAD_DIM ** (-0.5) * math.log2(math.e)
XF, SIB, OWN, ZP, ZM = range(5)
TO_ZP, TO_ZM, HAND = range(3)
YN, DG, XR = range(3)
R_Y, R_Z, R_SIB = range(3)
F_ZP, F_ZM, F_OWN, F_ZPY, F_NEAR, F_YN, F_DG, F_XR = range(8)
MESH = pl.DeviceIdType.MESH
GROUPS = (4, 3, 2, 2)
RELAYED = 1
SPANS = GROUPS + (RELAYED,)
FIRST = tuple(sum(SPANS[:g]) for g in range(len(SPANS)))
HELD = 4
EARLY = 1


def kernel(
    devices,
    picks_hbm,
    q_hbm,
    k_hbm,
    v_hbm,
    w_hbm,
    out,
    picks,
    picks_y,
    qv,
    qy,
    wv,
    kbuf,
    vbuf,
    krel,
    vrel,
    mult,
    top,
    tot,
    acc,
    give_o,
    give_l,
    take_o,
    take_l,
    mixed_heads,
    projected,
    kept,
    kept_sum,
    load_sem,
    send_z,
    recv_z,
    send_sib,
    recv_sib,
    send_y,
    recv_y,
    send_p,
    recv_p,
    send_r,
    recv_r,
):
    rows = q_hbm.shape[0]
    chips = devices // 2
    count = len(GROUPS)
    p = lax.axis_index("tm")
    chip = p // 2
    core = p % 2
    even = chip % 2 == 0
    step = jnp.where(even, 1, -1)
    has_p = (chip + 2 * step >= 0) & (chip + 2 * step < chips)
    has_m = (chip - 2 * step >= 0) & (chip - 2 * step < chips)
    gives = (core + chip) % 2 == 0
    takes = jnp.logical_not(gives)

    sib = p + 1 - 2 * core
    y_dev = p + 2 * step
    zp_dev = p + 4 * step
    zm_dev = p - 4 * step
    bufs = (kbuf, vbuf)
    hbms = (k_hbm, v_hbm)
    rels = (krel, vrel)

    def columns_of(g):
        return pl.ds(FIRST[g] * HEAD_DIM, SPANS[g] * HEAD_DIM)

    def slot(index):
        return pl.ds(index * rows, rows)

    def remote(src, dst, send, recv, dev):
        return pltpu.make_async_remote_copy(
            src_ref=src, dst_ref=dst, send_sem=send, recv_sem=recv, device_id={"tm": dev}, device_id_type=MESH
        )

    def along_z(kind, g, kv):
        dst, dev = ((ZM, zp_dev), (ZP, zm_dev), (XF, sib))[kind]
        columns = columns_of(g)
        src = bufs[kv].at[slot(ZP), columns] if kind == HAND else hbms[kv].at[:, columns]
        where = (kind, g, kv)
        return remote(src, bufs[kv].at[slot(dst), columns], send_z.at[where], recv_z.at[where], dev)

    def to_sib(kv):
        return remote(hbms[kv], bufs[kv].at[slot(SIB)], send_sib.at[kv], recv_sib.at[kv], sib)

    def to_y(kind, g):
        columns = columns_of(g)
        src, dst = (
            (q_hbm.at[:, columns], qy.at[:, columns]),
            (give_o.at[:, columns], take_o.at[:, columns]),
            (give_l.at[g], take_l.at[g]),
        )[kind]
        return remote(src, dst, send_y.at[kind, g], recv_y.at[kind, g], y_dev)

    def relayed(kind, kv, given=YN):
        src = hbms[kv].at[:, columns_of(count)] if kind == R_Y else rels[kv].at[slot(given)]
        dst, dev = ((YN, y_dev), (DG, zp_dev), (XR, sib))[kind]
        return remote(src, rels[kv].at[slot(dst)], send_r.at[kind, kv], recv_r.at[kind, kv], dev)

    picks_to_y = remote(picks_hbm, picks_y, send_p, recv_p, y_dev)
    load_w = pltpu.make_async_copy(w_hbm, wv, load_sem.at[4])
    load_picks = pltpu.make_async_copy(picks_hbm, picks, load_sem.at[3])
    barrier = pltpu.get_barrier_semaphore()

    def greet(dev):
        pl.semaphore_signal(barrier, inc=1, device_id={"tm": dev}, device_id_type=MESH)

    greet(sib)
    greet(y_dev)

    @pl.when(has_p)
    def _():
        greet(zp_dev)

    @pl.when(has_m)
    def _():
        greet(zm_dev)

    load_picks.start()
    loads = [
        pltpu.make_async_copy(q_hbm, qv, load_sem.at[0]),
        pltpu.make_async_copy(k_hbm, kbuf.at[slot(OWN)], load_sem.at[1]),
        pltpu.make_async_copy(v_hbm, vbuf.at[slot(OWN)], load_sem.at[2]),
    ]
    for load in loads:
        load.start()

    pl.semaphore_wait(barrier, 2 + jnp.where(has_p, 1, 0) + jnp.where(has_m, 1, 0))

    def send_zm(g):
        @pl.when(has_m)
        def _():
            for kv in range(2):
                along_z(TO_ZM, g, kv).start()

    def send_zp(g):
        @pl.when(has_p)
        def _():
            for kv in range(2):
                along_z(TO_ZP, g, kv).start()

    @pl.when(gives)
    def _():
        send_zm(0)

    for kv in range(2):
        relayed(R_Y, kv).start()
    send_zp(0)
    picks_to_y.start()
    to_y(0, 0).start()
    for kv in range(2):
        to_sib(kv).start()
    for g in range(1, count + 1):

        @pl.when(gives)
        def _():
            send_zm(g)

        if g < HELD:
            send_zp(g)
        if g < count:
            to_y(0, g).start()

    @pl.when(takes)
    def _():
        to_sib(0).wait_recv()
        for g in range(count + 1):
            send_zm(g)

    load_w.start()
    load_picks.wait()
    picks_to_y.wait_recv()

    ints = jnp.int32
    row_at = lax.broadcasted_iota(ints, (rows, rows), 0)
    col_at = lax.broadcasted_iota(ints, (rows, rows), 1)
    row_first = row_at < BLK
    col_first = col_at < BLK
    diagonal = row_at == col_at

    def fill(index, named, up, down, valid):
        one = jnp.where(valid, 1, 0)
        seconds = [
            jnp.where(even, named[b, up] + named[b, up + 1], named[b, down] + named[b, down + 1]) for b in range(2)
        ]
        cells = [[((2 - n) * one).astype(jnp.float32), (n * one).astype(jnp.float32)] for n in seconds]
        mult[index] = jnp.where(
            row_first,
            jnp.where(col_first, cells[0][0], cells[0][1]),
            jnp.where(col_first, cells[1][0], cells[1][1]),
        )

    near_valid = gives | has_p
    fill(F_ZP, picks, 6, 2, has_p)
    fill(F_ZM, picks, 2, 6, has_m)
    fill(F_OWN, picks_y, 0, 4, True)
    fill(F_ZPY, picks_y, 4, 0, has_p)
    fill(F_YN, picks, 4, 0, True)
    fill(F_DG, picks, 0, 4, has_m)
    over_valid = takes | has_m
    mult[F_XR] = jnp.full((rows, rows), jnp.where(over_valid, 1.0, 0.0), jnp.float32)
    mult[F_NEAR] = jnp.full((rows, rows), jnp.where(near_valid, 1.0, 0.0), jnp.float32)

    def clear(ref, index):
        ref[index * rows : (index + 1) * rows] = jnp.zeros((rows, ref.shape[1]), ref.dtype)

    @pl.when(jnp.logical_not(has_p))
    def _():
        clear(vbuf, ZP)

    @pl.when(jnp.logical_not(has_m))
    def _():
        clear(vbuf, ZM)
        clear(vrel, DG)

    @pl.when(jnp.logical_not(near_valid))
    def _():
        clear(vbuf, XF)

    @pl.when(jnp.logical_not(over_valid))
    def _():
        clear(vrel, XR)

    near = pl.ds(pl.multiple_of(jnp.where(gives, SIB, XF) * rows, rows), rows)

    def weigh(query, head, parts):
        columns = slice(head * HEAD_DIM, (head + 1) * HEAD_DIM)
        pieces = []
        for k_from, _, factors in parts:
            scores = lax.dot_general(
                query[:, columns],
                k_from[...],
                (((1,), (1,)), ((), ())),
                preferred_element_type=jnp.float32,
            )
            for i, factor in enumerate(factors):
                piece = scores[:, i * rows : (i + 1) * rows]
                if factor is not None:
                    piece = jnp.where(mult[factor] > 0, piece, NEG)
                pieces.append((piece, factor))
        high = functools.reduce(jnp.maximum, [piece for piece, _ in pieces])
        high = jnp.broadcast_to(jnp.max(high, axis=1, keepdims=True), high.shape)
        weights = []
        for piece, factor in pieces:
            weight = jnp.exp2((piece - high) * EXP_SCALE)
            if factor is not None:
                weight = weight * mult[factor]
            weights.append(weight)
        summed = functools.reduce(jnp.add, weights)
        summed = jnp.broadcast_to(jnp.sum(summed, axis=1, keepdims=True), summed.shape)
        return high * EXP_SCALE, summed, [weight.astype(jnp.bfloat16) for weight in weights]

    def gather(weights, parts):
        mixed = None
        for _, v_from, factors in parts:
            now, weights = weights[: len(factors)], weights[len(factors) :]
            now = jnp.concatenate(now, axis=1)
            term = jnp.dot(now, v_from[...], preferred_element_type=jnp.float32)
            mixed = term if mixed is None else mixed + term
        return mixed

    def held(where, head, factors):
        columns = pl.ds(head * HEAD_DIM, HEAD_DIM)
        return kbuf.at[where, columns], vbuf.at[where, columns], factors

    def help_parts(head):
        return held(near, head, (F_NEAR,)), held(pl.ds(OWN * rows, 2 * rows), head, (F_OWN, F_ZPY))

    def heads_of(g):
        return range(FIRST[g], FIRST[g] + SPANS[g])

    def help_weigh(g):
        found = [weigh(qy, head, help_parts(head)) for head in heads_of(g)]
        for j, (high, summed, _) in enumerate(found):
            size = high + jnp.log2(summed)
            give_l[g, j : j + 1] = jnp.sum(jnp.where(diagonal, size, 0.0), axis=0, keepdims=True)
        return found

    def help_gather(g, found):
        for head, (_, summed, weights) in zip(heads_of(g), found):
            columns = slice(head * HEAD_DIM, (head + 1) * HEAD_DIM)
            mixed = gather(weights, help_parts(head))
            give_o[:, columns] = (mixed / summed).astype(give_o.dtype)

    def near_part(head):
        return held(pl.ds(SIB * rows, 4 * rows), head, (None, None, F_ZP, F_ZM))

    def local_weigh(g):
        found = [weigh(qv, head, (near_part(head),)) for head in heads_of(g)]
        for head, (high, summed, _) in zip(heads_of(g), found):
            top[head], tot[head] = high, summed
        return [weights for _, _, weights in found]

    def local_gather(g, found):
        for head, weights in zip(heads_of(g), found):
            acc[head] = gather(weights, (near_part(head),))

    def relayed_parts(head):
        mine = pl.ds((head - FIRST[count]) * HEAD_DIM, HEAD_DIM)
        return near_part(head), (krel.at[:, mine], vrel.at[:, mine], (F_YN, F_DG, F_XR))

    def relayed_ready(kv):
        @pl.when(has_p)
        def _():
            along_z(TO_ZM, count, kv).wait_recv()

        below_ready(count, kv)

        @pl.when(over_valid)
        def _():
            relayed(R_SIB, kv).wait_recv()

    def relayed_weigh():
        return [weigh(qv, head, relayed_parts(head)) for head in heads_of(count)]

    def relayed_gather(found):
        for head, (_, summed, weights) in zip(heads_of(count), found):
            columns = slice(head * HEAD_DIM, (head + 1) * HEAD_DIM)
            mixed = gather(weights, relayed_parts(head))
            mixed_heads[:, columns] = (mixed / summed).astype(mixed_heads.dtype)

    def returned(g):
        for kind in (1, 2):
            to_y(kind, g).wait_recv()

    def merge_group(g):
        for j in range(GROUPS[g]):
            head = FIRST[g] + j
            columns = slice(head * HEAD_DIM, (head + 1) * HEAD_DIM)
            size = jnp.broadcast_to(take_l[g, j : j + 1], (rows, rows))
            size = jnp.sum(jnp.where(diagonal, size, 0.0), axis=1, keepdims=True)
            size = jnp.broadcast_to(size, (rows, rows))
            high = jnp.maximum(top[head], size)
            mine = jnp.exp2(top[head] - high)
            theirs = jnp.exp2(size - high)
            mixed = acc[head] * mine + take_o[:, columns].astype(jnp.float32) * theirs
            mixed_heads[:, columns] = (mixed / (tot[head] * mine + theirs)).astype(mixed_heads.dtype)

    for load in loads:
        load.wait()

    @pl.when(gives)
    def _():
        to_sib(0).wait_recv()

    to_sib(1).wait_recv()
    def relay():
        for kv in range(2):
            relayed(R_Y, kv).wait_recv()

        @pl.when(has_p)
        def _():
            for kv in range(2):
                relayed(R_Z, kv).start()

        for g in range(HELD, count + 1):
            send_zp(g)

        @pl.when(gives)
        def _():
            for kv in range(2):
                relayed(R_SIB, kv).start()

    def above_ready(g, kv):
        @pl.when(has_p)
        def _():
            along_z(TO_ZM, g, kv).wait_recv()

        @pl.when(has_p & gives)
        def _():
            along_z(HAND, g, kv).start()

    def handed(g, kv):
        @pl.when(has_p & takes)
        def _():
            along_z(HAND, g, kv).wait_recv()

    def below_ready(g, kv):
        @pl.when(has_m)
        def _():
            along_z(TO_ZP, g, kv).wait_recv()

    def project(first, end):
        rows_of = slice(FIRST[first] * HEAD_DIM, (FIRST[end - 1] + SPANS[end - 1]) * HEAD_DIM)
        return jnp.dot(mixed_heads[:, rows_of], wv[rows_of], preferred_element_type=jnp.float32)

    def give(g):
        for kind in (1, 2):
            to_y(kind, g).start()

    final = count - 1
    for g in range(count):
        if g == final:
            load_w.wait()
            for done in range(EARLY):
                returned(done)
            for done in range(EARLY):
                merge_group(done)
            projected[...] = project(0, EARLY)
        if g > 0:
            below_ready(g - 1, 1)
            local_gather(g - 1, nearby)
        above_ready(g, 0)
        handed(g, 0)
        if g < final:
            to_y(0, g).wait_recv()
            found = help_weigh(g)
        else:

            @pl.when(has_p)
            def _():
                to_y(0, final).wait_recv()
                for j, (_, summed, weights) in enumerate(help_weigh(final)):
                    kept_sum[j] = summed
                    for i, weight in enumerate(weights):
                        kept[j, i] = weight

        below_ready(g, 0)
        nearby = local_weigh(g)
        above_ready(g, 1)
        handed(g, 1)
        if g < final:
            help_gather(g, found)
            give(g)
        else:

            @pl.when(has_p)
            def _():
                help_gather(final, [(None, kept_sum[j], [kept[j, i] for i in range(3)]) for j in range(GROUPS[final])])
                give(final)

        if g == 1:
            relay()

            @pl.when(jnp.logical_not(has_p))
            def _():
                to_y(0, final).wait_recv()
                help_gather(final, help_weigh(final))
                give(final)

    below_ready(final, 1)
    for g in range(EARLY, final):
        returned(g)
    local_gather(final, nearby)
    for g in range(EARLY, final):
        merge_group(g)
    projected[...] += project(EARLY, final)

    @pl.when(has_m)
    def _():
        for kv in range(2):
            relayed(R_Z, kv).wait_recv()

    @pl.when(has_m & takes)
    def _():
        for kv in range(2):
            relayed(R_SIB, kv, DG).start()

    relayed_ready(0)
    found = relayed_weigh()
    relayed_ready(1)

    def sends_done(first, end):
        for kind, sent in ((TO_ZP, has_p), (TO_ZM, has_m)):

            @pl.when(sent)
            def _():
                for g in range(first, end):
                    for kv in range(2):
                        along_z(kind, g, kv).wait_send()

    picks_to_y.wait_send()
    for kv in range(2):
        to_sib(kv).wait_send()
        relayed(R_Y, kv).wait_send()
    for g in range(count):
        for kind in range(3 if g < count - 1 else 1):
            to_y(kind, g).wait_send()

    @pl.when(has_p & gives)
    def _():
        for g in range(count - 1):
            for kv in range(2):
                along_z(HAND, g, kv).wait_send()

    sends_done(0, 1)

    returned(final)
    relayed_gather(found)
    merge_group(final)
    out[...] = (projected[...] + project(count - 1, count + 1)).astype(out.dtype)
    for kind in (1, 2):
        to_y(kind, count - 1).wait_send()
    sends_done(1, count + 1)

    @pl.when(has_p)
    def _():
        for kv in range(2):
            relayed(R_Z, kv).wait_send()

    @pl.when(gives | has_m)
    def _():
        for kv in range(2):
            relayed(R_SIB, kv).wait_send()

    @pl.when(has_p & gives)
    def _():
        for kv in range(2):
            along_z(HAND, count - 1, kv).wait_send()


def attention(devices, queries, keys, values, far_picks, out_weight):
    rows, width = queries.shape
    count = len(GROUPS)
    in_hbm = pl.BlockSpec(memory_space=pltpu.HBM)
    per_head = pltpu.VMEM((HEADS, rows, HEAD_DIM), jnp.float32)
    wide = pltpu.VMEM((rows, width), jnp.bfloat16)
    sizes = pltpu.VMEM((count, 8, rows), jnp.float32)
    over = pltpu.VMEM((3 * rows, RELAYED * HEAD_DIM), jnp.bfloat16)
    dma = pltpu.SemaphoreType.DMA
    return pl.pallas_call(
        functools.partial(kernel, devices),
        out_shape=jax.ShapeDtypeStruct((rows, width), jnp.bfloat16),
        in_specs=[in_hbm] * 5,
        out_specs=pl.BlockSpec(memory_space=pltpu.VMEM),
        scratch_shapes=[
            pltpu.SMEM(far_picks.shape, jnp.int32),
            pltpu.SMEM(far_picks.shape, jnp.int32),
            wide,
            wide,
            pltpu.VMEM(out_weight.shape, jnp.bfloat16),
            pltpu.VMEM((5 * rows, width), jnp.bfloat16),
            pltpu.VMEM((5 * rows, width), jnp.bfloat16),
            over,
            over,
            pltpu.VMEM((8, rows, rows), jnp.float32),
            per_head,
            per_head,
            per_head,
            wide,
            sizes,
            wide,
            sizes,
            wide,
            pltpu.VMEM((rows, width), jnp.float32),
            pltpu.VMEM((GROUPS[-1], 3, rows, rows), jnp.bfloat16),
            pltpu.VMEM((GROUPS[-1], rows, HEAD_DIM), jnp.float32),
            dma((5,)),
            dma((3, count + 1, 2)),
            dma((3, count + 1, 2)),
            dma((2,)),
            dma((2,)),
            dma((3, count)),
            dma((3, count)),
            dma,
            dma,
            dma((3, 2)),
            dma((3, 2)),
        ],
        compiler_params=pltpu.CompilerParams(
            collective_id=0, has_side_effects=True, vmem_limit_bytes=56_000_000
        ),
        name="helper_attention",
    )(*(pltpu.with_memory_space_constraint(x, pltpu.HBM) for x in (far_picks, queries, keys, values, out_weight)))


def solution(mesh):
    devices = mesh.shape["tm"]

    def body(queries, keys, values, far_picks, out_weight):
        return attention(devices, queries, keys, values, far_picks, out_weight)

    placed = (
        P(("vid", "tm"), None),
        P(("vid", "tm"), None),
        P(("vid", "tm"), None),
        P(("vid", "tm"), None),
        P(),
    )
    return jax.shard_map(
        body, mesh=mesh, in_specs=placed, out_specs=P(("vid", "tm"), None), check_vma=False
    )
```

```python
import functools
import math

import jax
import jax.numpy as jnp
from jax import lax
from jax.experimental import pallas as pl
from jax.experimental.pallas import tpu as pltpu
from jax.sharding import PartitionSpec as P

HEADS = 12
HEAD_DIM = 128
BLK = 64
NEG = -1e30
EXP_SCALE = HEAD_DIM ** (-0.5) * math.log2(math.e)
XF, SIB, OWN, ZP, ZM = range(5)
TO_ZP, TO_ZM, HAND = range(3)
YN, DG, XR = range(3)
R_Y, R_Z, R_SIB = range(3)
F_ZP, F_ZM, F_OWN, F_ZPY, F_NEAR, F_YN, F_DG, F_XR = range(8)
MESH = pl.DeviceIdType.MESH
GROUPS = (4, 4, 3)
RELAYED = 1
SPANS = GROUPS + (RELAYED,)
FIRST = tuple(sum(SPANS[:g]) for g in range(len(SPANS)))
HELD = 3
EARLY = 1


def kernel(
    devices,
    picks_hbm,
    q_hbm,
    k_hbm,
    v_hbm,
    w_hbm,
    out,
    picks,
    picks_y,
    qv,
    qy,
    wv,
    kbuf,
    vbuf,
    krel,
    vrel,
    mult,
    top,
    tot,
    acc,
    give_o,
    give_l,
    take_o,
    take_l,
    mixed_heads,
    projected,
    kept,
    kept_sum,
    load_sem,
    send_z,
    recv_z,
    send_sib,
    recv_sib,
    send_y,
    recv_y,
    send_p,
    recv_p,
    send_r,
    recv_r,
):
    rows = q_hbm.shape[0]
    chips = devices // 2
    count = len(GROUPS)
    p = lax.axis_index("tm")
    chip = p // 2
    core = p % 2
    even = chip % 2 == 0
    step = jnp.where(even, 1, -1)
    has_p = (chip + 2 * step >= 0) & (chip + 2 * step < chips)
    has_m = (chip - 2 * step >= 0) & (chip - 2 * step < chips)
    gives = (core + chip) % 2 == 0
    takes = jnp.logical_not(gives)

    sib = p + 1 - 2 * core
    y_dev = p + 2 * step
    zp_dev = p + 4 * step
    zm_dev = p - 4 * step
    bufs = (kbuf, vbuf)
    hbms = (k_hbm, v_hbm)
    rels = (krel, vrel)

    def columns_of(g):
        return pl.ds(FIRST[g] * HEAD_DIM, SPANS[g] * HEAD_DIM)

    def slot(index):
        return pl.ds(index * rows, rows)

    def remote(src, dst, send, recv, dev):
        return pltpu.make_async_remote_copy(
            src_ref=src, dst_ref=dst, send_sem=send, recv_sem=recv, device_id={"tm": dev}, device_id_type=MESH
        )

    def along_z(kind, g, kv):
        dst, dev = ((ZM, zp_dev), (ZP, zm_dev), (XF, sib))[kind]
        columns = columns_of(g)
        src = bufs[kv].at[slot(ZP), columns] if kind == HAND else hbms[kv].at[:, columns]
        where = (kind, g, kv)
        return remote(src, bufs[kv].at[slot(dst), columns], send_z.at[where], recv_z.at[where], dev)

    def to_sib(kv):
        return remote(hbms[kv], bufs[kv].at[slot(SIB)], send_sib.at[kv], recv_sib.at[kv], sib)

    def to_y(kind, g):
        columns = columns_of(g)
        src, dst = (
            (q_hbm.at[:, columns], qy.at[:, columns]),
            (give_o.at[:, columns], take_o.at[:, columns]),
            (give_l.at[g], take_l.at[g]),
        )[kind]
        return remote(src, dst, send_y.at[kind, g], recv_y.at[kind, g], y_dev)

    def relayed(kind, kv, given=YN):
        src = hbms[kv].at[:, columns_of(count)] if kind == R_Y else rels[kv].at[slot(given)]
        dst, dev = ((YN, y_dev), (DG, zp_dev), (XR, sib))[kind]
        return remote(src, rels[kv].at[slot(dst)], send_r.at[kind, kv], recv_r.at[kind, kv], dev)

    picks_to_y = remote(picks_hbm, picks_y, send_p, recv_p, y_dev)
    load_w = pltpu.make_async_copy(w_hbm, wv, load_sem.at[4])
    load_picks = pltpu.make_async_copy(picks_hbm, picks, load_sem.at[3])
    barrier = pltpu.get_barrier_semaphore()

    def greet(dev):
        pl.semaphore_signal(barrier, inc=1, device_id={"tm": dev}, device_id_type=MESH)

    greet(sib)
    greet(y_dev)

    @pl.when(has_p)
    def _():
        greet(zp_dev)

    @pl.when(has_m)
    def _():
        greet(zm_dev)

    load_picks.start()
    loads = [
        pltpu.make_async_copy(q_hbm, qv, load_sem.at[0]),
        pltpu.make_async_copy(k_hbm, kbuf.at[slot(OWN)], load_sem.at[1]),
        pltpu.make_async_copy(v_hbm, vbuf.at[slot(OWN)], load_sem.at[2]),
    ]
    for load in loads:
        load.start()

    pl.semaphore_wait(barrier, 2 + jnp.where(has_p, 1, 0) + jnp.where(has_m, 1, 0))

    def send_zm(g):
        @pl.when(has_m)
        def _():
            for kv in range(2):
                along_z(TO_ZM, g, kv).start()

    def send_zp(g):
        @pl.when(has_p)
        def _():
            for kv in range(2):
                along_z(TO_ZP, g, kv).start()

    @pl.when(gives)
    def _():
        send_zm(0)

    send_zp(0)
    picks_to_y.start()
    to_y(0, 0).start()
    for kv in range(2):
        relayed(R_Y, kv).start()
    for kv in range(2):
        to_sib(kv).start()
    for g in range(1, count + 1):

        if g < count:

            @pl.when(gives)
            def _():
                send_zm(g)

        if g < HELD:
            send_zp(g)
        if g < count:
            to_y(0, g).start()

    @pl.when(takes)
    def _():
        to_sib(0).wait_recv()
        for g in range(count + 1):
            send_zm(g)

    load_w.start()
    load_picks.wait()
    picks_to_y.wait_recv()

    ints = jnp.int32
    row_at = lax.broadcasted_iota(ints, (rows, rows), 0)
    col_at = lax.broadcasted_iota(ints, (rows, rows), 1)
    row_first = row_at < BLK
    col_first = col_at < BLK
    diagonal = row_at == col_at

    def fill(index, named, up, down, valid):
        one = jnp.where(valid, 1, 0)
        seconds = [
            jnp.where(even, named[b, up] + named[b, up + 1], named[b, down] + named[b, down + 1]) for b in range(2)
        ]
        cells = [[((2 - n) * one).astype(jnp.float32), (n * one).astype(jnp.float32)] for n in seconds]
        mult[index] = jnp.where(
            row_first,
            jnp.where(col_first, cells[0][0], cells[0][1]),
            jnp.where(col_first, cells[1][0], cells[1][1]),
        )

    near_valid = gives | has_p
    fill(F_ZP, picks, 6, 2, has_p)
    fill(F_ZM, picks, 2, 6, has_m)
    fill(F_OWN, picks_y, 0, 4, True)
    fill(F_ZPY, picks_y, 4, 0, has_p)
    fill(F_YN, picks, 4, 0, True)
    fill(F_DG, picks, 0, 4, has_m)
    over_valid = takes | has_m
    mult[F_XR] = jnp.full((rows, rows), jnp.where(over_valid, 1.0, 0.0), jnp.float32)
    mult[F_NEAR] = jnp.full((rows, rows), jnp.where(near_valid, 1.0, 0.0), jnp.float32)

    def clear(ref, index):
        ref[index * rows : (index + 1) * rows] = jnp.zeros((rows, ref.shape[1]), ref.dtype)

    @pl.when(jnp.logical_not(has_p))
    def _():
        clear(vbuf, ZP)

    @pl.when(jnp.logical_not(has_m))
    def _():
        clear(vbuf, ZM)
        clear(vrel, DG)

    @pl.when(jnp.logical_not(near_valid))
    def _():
        clear(vbuf, XF)

    @pl.when(jnp.logical_not(over_valid))
    def _():
        clear(vrel, XR)

    near = pl.ds(pl.multiple_of(jnp.where(gives, SIB, XF) * rows, rows), rows)

    def weigh(query, head, parts):
        columns = slice(head * HEAD_DIM, (head + 1) * HEAD_DIM)
        pieces = []
        for k_from, _, factors in parts:
            scores = lax.dot_general(
                query[:, columns],
                k_from[...],
                (((1,), (1,)), ((), ())),
                preferred_element_type=jnp.float32,
            )
            for i, factor in enumerate(factors):
                piece = scores[:, i * rows : (i + 1) * rows]
                if factor is not None:
                    piece = jnp.where(mult[factor] > 0, piece, NEG)
                pieces.append((piece, factor))
        high = functools.reduce(jnp.maximum, [piece for piece, _ in pieces])
        high = jnp.broadcast_to(jnp.max(high, axis=1, keepdims=True), high.shape)
        weights = []
        for piece, factor in pieces:
            weight = jnp.exp2((piece - high) * EXP_SCALE)
            if factor is not None:
                weight = weight * mult[factor]
            weights.append(weight)
        summed = functools.reduce(jnp.add, weights)
        summed = jnp.broadcast_to(jnp.sum(summed, axis=1, keepdims=True), summed.shape)
        return high * EXP_SCALE, summed, [weight.astype(jnp.bfloat16) for weight in weights]

    def gather(weights, parts):
        mixed = None
        for _, v_from, factors in parts:
            now, weights = weights[: len(factors)], weights[len(factors) :]
            now = jnp.concatenate(now, axis=1)
            term = jnp.dot(now, v_from[...], preferred_element_type=jnp.float32)
            mixed = term if mixed is None else mixed + term
        return mixed

    def held(where, head, factors):
        columns = pl.ds(head * HEAD_DIM, HEAD_DIM)
        return kbuf.at[where, columns], vbuf.at[where, columns], factors

    def help_parts(head):
        return held(near, head, (F_NEAR,)), held(pl.ds(OWN * rows, 2 * rows), head, (F_OWN, F_ZPY))

    def heads_of(g):
        return range(FIRST[g], FIRST[g] + SPANS[g])

    def help_weigh(g):
        found = [weigh(qy, head, help_parts(head)) for head in heads_of(g)]
        for j, (high, summed, _) in enumerate(found):
            size = high + jnp.log2(summed)
            give_l[g, j : j + 1] = jnp.sum(jnp.where(diagonal, size, 0.0), axis=0, keepdims=True)
        return found

    def help_gather(g, found):
        for head, (_, summed, weights) in zip(heads_of(g), found):
            columns = slice(head * HEAD_DIM, (head + 1) * HEAD_DIM)
            mixed = gather(weights, help_parts(head))
            give_o[:, columns] = (mixed / summed).astype(give_o.dtype)

    def near_part(head):
        return held(pl.ds(SIB * rows, 4 * rows), head, (None, None, F_ZP, F_ZM))

    def local_weigh(g):
        found = [weigh(qv, head, (near_part(head),)) for head in heads_of(g)]
        for head, (high, summed, _) in zip(heads_of(g), found):
            top[head], tot[head] = high, summed
        return [weights for _, _, weights in found]

    def local_gather(g, found):
        for head, weights in zip(heads_of(g), found):
            acc[head] = gather(weights, (near_part(head),))

    def relayed_parts(head):
        mine = pl.ds((head - FIRST[count]) * HEAD_DIM, HEAD_DIM)
        return near_part(head), (krel.at[:, mine], vrel.at[:, mine], (F_YN, F_DG, F_XR))

    def relayed_ready(kv):
        @pl.when(has_p)
        def _():
            along_z(TO_ZM, count, kv).wait_recv()

        below_ready(count, kv)

        @pl.when(over_valid)
        def _():
            relayed(R_SIB, kv).wait_recv()

    def relayed_weigh():
        return [weigh(qv, head, relayed_parts(head)) for head in heads_of(count)]

    def relayed_gather(found):
        for head, (_, summed, weights) in zip(heads_of(count), found):
            columns = slice(head * HEAD_DIM, (head + 1) * HEAD_DIM)
            mixed = gather(weights, relayed_parts(head))
            mixed_heads[:, columns] = (mixed / summed).astype(mixed_heads.dtype)

    def returned(g):
        for kind in (1, 2):
            to_y(kind, g).wait_recv()

    def merge_group(g):
        for j in range(GROUPS[g]):
            head = FIRST[g] + j
            columns = slice(head * HEAD_DIM, (head + 1) * HEAD_DIM)
            size = jnp.broadcast_to(take_l[g, j : j + 1], (rows, rows))
            size = jnp.sum(jnp.where(diagonal, size, 0.0), axis=1, keepdims=True)
            size = jnp.broadcast_to(size, (rows, rows))
            high = jnp.maximum(top[head], size)
            mine = jnp.exp2(top[head] - high)
            theirs = jnp.exp2(size - high)
            mixed = acc[head] * mine + take_o[:, columns].astype(jnp.float32) * theirs
            mixed_heads[:, columns] = (mixed / (tot[head] * mine + theirs)).astype(mixed_heads.dtype)

    for load in loads:
        load.wait()

    @pl.when(gives)
    def _():
        to_sib(0).wait_recv()

    to_sib(1).wait_recv()
    def relay():
        for kv in range(2):
            relayed(R_Y, kv).wait_recv()

        @pl.when(has_p)
        def _():
            for kv in range(2):
                relayed(R_Z, kv).start()

        for g in range(HELD, count + 1):
            send_zp(g)

        @pl.when(gives)
        def _():
            for kv in range(2):
                relayed(R_SIB, kv).start()

    def above_ready(g, kv):
        @pl.when(has_p)
        def _():
            along_z(TO_ZM, g, kv).wait_recv()

        @pl.when(has_p & gives)
        def _():
            along_z(HAND, g, kv).start()

    def handed(g, kv):
        @pl.when(has_p & takes)
        def _():
            along_z(HAND, g, kv).wait_recv()

    def below_ready(g, kv):
        @pl.when(has_m)
        def _():
            along_z(TO_ZP, g, kv).wait_recv()

    def project(first, end):
        rows_of = slice(FIRST[first] * HEAD_DIM, (FIRST[end - 1] + SPANS[end - 1]) * HEAD_DIM)
        return jnp.dot(mixed_heads[:, rows_of], wv[rows_of], preferred_element_type=jnp.float32)

    def give(g):
        for kind in (1, 2):
            to_y(kind, g).start()

    final = count - 1
    for g in range(count):
        if g == final:
            load_w.wait()
            for done in range(EARLY):
                returned(done)
            for done in range(EARLY):
                merge_group(done)
            projected[...] = project(0, EARLY)
        if g > 0:
            below_ready(g - 1, 1)
            local_gather(g - 1, nearby)
        if g == final:

            @pl.when(gives)
            def _():
                send_zm(count)

        above_ready(g, 0)
        handed(g, 0)
        if g < final:
            to_y(0, g).wait_recv()
            found = help_weigh(g)
        else:

            @pl.when(has_p)
            def _():
                to_y(0, final).wait_recv()
                for j, (_, summed, weights) in enumerate(help_weigh(final)):
                    kept_sum[j] = summed
                    for i, weight in enumerate(weights):
                        kept[j, i] = weight

        below_ready(g, 0)
        nearby = local_weigh(g)
        above_ready(g, 1)
        handed(g, 1)
        if g < final:
            help_gather(g, found)
            give(g)
        else:

            @pl.when(has_p)
            def _():
                help_gather(final, [(None, kept_sum[j], [kept[j, i] for i in range(3)]) for j in range(GROUPS[final])])
                give(final)

        if g == 0:
            relay()
        if g == 1:

            @pl.when(jnp.logical_not(has_p))
            def _():
                to_y(0, final).wait_recv()
                help_gather(final, help_weigh(final))
                give(final)

    below_ready(final, 1)
    for g in range(EARLY, final):
        returned(g)
    local_gather(final, nearby)
    for g in range(EARLY, final):
        merge_group(g)
    projected[...] += project(EARLY, final)

    @pl.when(has_m)
    def _():
        for kv in range(2):
            relayed(R_Z, kv).wait_recv()

    @pl.when(has_m & takes)
    def _():
        for kv in range(2):
            relayed(R_SIB, kv, DG).start()

    relayed_ready(0)
    found = relayed_weigh()
    relayed_ready(1)

    def sends_done(first, end):
        for kind, sent in ((TO_ZP, has_p), (TO_ZM, has_m)):

            @pl.when(sent)
            def _():
                for g in range(first, end):
                    for kv in range(2):
                        along_z(kind, g, kv).wait_send()

    picks_to_y.wait_send()
    for kv in range(2):
        to_sib(kv).wait_send()
        relayed(R_Y, kv).wait_send()
    for g in range(count):
        for kind in range(3 if g < count - 1 else 1):
            to_y(kind, g).wait_send()

    @pl.when(has_p & gives)
    def _():
        for g in range(count - 1):
            for kv in range(2):
                along_z(HAND, g, kv).wait_send()

    sends_done(0, 1)

    returned(final)
    relayed_gather(found)
    merge_group(final)
    out[...] = (projected[...] + project(count - 1, count + 1)).astype(out.dtype)
    for kind in (1, 2):
        to_y(kind, count - 1).wait_send()
    sends_done(1, count + 1)

    @pl.when(has_p)
    def _():
        for kv in range(2):
            relayed(R_Z, kv).wait_send()

    @pl.when(gives | has_m)
    def _():
        for kv in range(2):
            relayed(R_SIB, kv).wait_send()

    @pl.when(has_p & gives)
    def _():
        for kv in range(2):
            along_z(HAND, count - 1, kv).wait_send()


def attention(devices, queries, keys, values, far_picks, out_weight):
    rows, width = queries.shape
    count = len(GROUPS)
    in_hbm = pl.BlockSpec(memory_space=pltpu.HBM)
    per_head = pltpu.VMEM((HEADS, rows, HEAD_DIM), jnp.float32)
    wide = pltpu.VMEM((rows, width), jnp.bfloat16)
    sizes = pltpu.VMEM((count, 8, rows), jnp.float32)
    over = pltpu.VMEM((3 * rows, RELAYED * HEAD_DIM), jnp.bfloat16)
    dma = pltpu.SemaphoreType.DMA
    return pl.pallas_call(
        functools.partial(kernel, devices),
        out_shape=jax.ShapeDtypeStruct((rows, width), jnp.bfloat16),
        in_specs=[in_hbm] * 5,
        out_specs=pl.BlockSpec(memory_space=pltpu.VMEM),
        scratch_shapes=[
            pltpu.SMEM(far_picks.shape, jnp.int32),
            pltpu.SMEM(far_picks.shape, jnp.int32),
            wide,
            wide,
            pltpu.VMEM(out_weight.shape, jnp.bfloat16),
            pltpu.VMEM((5 * rows, width), jnp.bfloat16),
            pltpu.VMEM((5 * rows, width), jnp.bfloat16),
            over,
            over,
            pltpu.VMEM((8, rows, rows), jnp.float32),
            per_head,
            per_head,
            per_head,
            wide,
            sizes,
            wide,
            sizes,
            wide,
            pltpu.VMEM((rows, width), jnp.float32),
            pltpu.VMEM((GROUPS[-1], 3, rows, rows), jnp.bfloat16),
            pltpu.VMEM((GROUPS[-1], rows, HEAD_DIM), jnp.float32),
            dma((5,)),
            dma((3, count + 1, 2)),
            dma((3, count + 1, 2)),
            dma((2,)),
            dma((2,)),
            dma((3, count)),
            dma((3, count)),
            dma,
            dma,
            dma((3, 2)),
            dma((3, 2)),
        ],
        compiler_params=pltpu.CompilerParams(
            collective_id=0, has_side_effects=True, vmem_limit_bytes=56_000_000
        ),
        name="helper_attention",
    )(*(pltpu.with_memory_space_constraint(x, pltpu.HBM) for x in (far_picks, queries, keys, values, out_weight)))


def solution(mesh):
    devices = mesh.shape["tm"]

    def body(queries, keys, values, far_picks, out_weight):
        return attention(devices, queries, keys, values, far_picks, out_weight)

    placed = (
        P(("vid", "tm"), None),
        P(("vid", "tm"), None),
        P(("vid", "tm"), None),
        P(("vid", "tm"), None),
        P(),
    )
    return jax.shard_map(
        body, mesh=mesh, in_specs=placed, out_specs=P(("vid", "tm"), None), check_vma=False
    )
```

```python
import functools
import math

import jax
import jax.numpy as jnp
from jax import lax
from jax.experimental import pallas as pl
from jax.experimental.pallas import tpu as pltpu
from jax.sharding import PartitionSpec as P

HEADS = 12
HEAD_DIM = 128
BLK = 64
NEG = -1e30
EXP_SCALE = HEAD_DIM ** (-0.5) * math.log2(math.e)
XF, SIB, OWN, ZP, ZM = range(5)
TO_ZP, TO_ZM, HAND = range(3)
YN, DG, XR = range(3)
R_Y, R_Z, R_SIB = range(3)
F_ZP, F_ZM, F_OWN, F_ZPY, F_NEAR, F_YN, F_DG, F_XR = range(8)
MESH = pl.DeviceIdType.MESH
GROUPS = (4, 4, 3)
RELAYED = 1
SPANS = GROUPS + (RELAYED,)
FIRST = tuple(sum(SPANS[:g]) for g in range(len(SPANS)))
HELD = 3
EARLY = 1


def kernel(
    devices,
    picks_hbm,
    q_hbm,
    k_hbm,
    v_hbm,
    w_hbm,
    out,
    picks,
    picks_y,
    qv,
    qy,
    wv,
    kbuf,
    vbuf,
    krel,
    vrel,
    mult,
    top,
    tot,
    acc,
    give_o,
    give_l,
    take_o,
    take_l,
    mixed_heads,
    projected,
    kept,
    kept_sum,
    load_sem,
    send_z,
    recv_z,
    send_sib,
    recv_sib,
    send_y,
    recv_y,
    send_p,
    recv_p,
    send_r,
    recv_r,
):
    rows = q_hbm.shape[0]
    chips = devices // 2
    count = len(GROUPS)
    p = lax.axis_index("tm")
    chip = p // 2
    core = p % 2
    even = chip % 2 == 0
    step = jnp.where(even, 1, -1)
    has_p = (chip + 2 * step >= 0) & (chip + 2 * step < chips)
    has_m = (chip - 2 * step >= 0) & (chip - 2 * step < chips)
    gives = (core + chip) % 2 == 0
    takes = jnp.logical_not(gives)

    sib = p + 1 - 2 * core
    y_dev = p + 2 * step
    zp_dev = p + 4 * step
    zm_dev = p - 4 * step
    bufs = (kbuf, vbuf)
    hbms = (k_hbm, v_hbm)
    rels = (krel, vrel)

    def columns_of(g):
        return pl.ds(FIRST[g] * HEAD_DIM, SPANS[g] * HEAD_DIM)

    def slot(index):
        return pl.ds(index * rows, rows)

    def remote(src, dst, send, recv, dev):
        return pltpu.make_async_remote_copy(
            src_ref=src, dst_ref=dst, send_sem=send, recv_sem=recv, device_id={"tm": dev}, device_id_type=MESH
        )

    def along_z(kind, g, kv):
        dst, dev = ((ZM, zp_dev), (ZP, zm_dev), (XF, sib))[kind]
        columns = columns_of(g)
        src = bufs[kv].at[slot(ZP), columns] if kind == HAND else hbms[kv].at[:, columns]
        where = (kind, g, kv)
        return remote(src, bufs[kv].at[slot(dst), columns], send_z.at[where], recv_z.at[where], dev)

    def to_sib(kv):
        return remote(hbms[kv], bufs[kv].at[slot(SIB)], send_sib.at[kv], recv_sib.at[kv], sib)

    def to_y(kind, g):
        columns = columns_of(g)
        src, dst = (
            (q_hbm.at[:, columns], qy.at[:, columns]),
            (give_o.at[:, columns], take_o.at[:, columns]),
            (give_l.at[g], take_l.at[g]),
        )[kind]
        return remote(src, dst, send_y.at[kind, g], recv_y.at[kind, g], y_dev)

    def relayed(kind, kv, given=YN):
        src = hbms[kv].at[:, columns_of(count)] if kind == R_Y else rels[kv].at[slot(given)]
        dst, dev = ((YN, y_dev), (DG, zp_dev), (XR, sib))[kind]
        return remote(src, rels[kv].at[slot(dst)], send_r.at[kind, kv], recv_r.at[kind, kv], dev)

    picks_to_y = remote(picks_hbm, picks_y, send_p, recv_p, y_dev)
    load_w = pltpu.make_async_copy(w_hbm, wv, load_sem.at[4])
    load_picks = pltpu.make_async_copy(picks_hbm, picks, load_sem.at[3])
    barrier = pltpu.get_barrier_semaphore()

    def greet(dev):
        pl.semaphore_signal(barrier, inc=1, device_id={"tm": dev}, device_id_type=MESH)

    greet(sib)
    greet(y_dev)

    @pl.when(has_p)
    def _():
        greet(zp_dev)

    @pl.when(has_m)
    def _():
        greet(zm_dev)

    load_picks.start()
    loads = [
        pltpu.make_async_copy(q_hbm, qv, load_sem.at[0]),
        pltpu.make_async_copy(k_hbm, kbuf.at[slot(OWN)], load_sem.at[1]),
        pltpu.make_async_copy(v_hbm, vbuf.at[slot(OWN)], load_sem.at[2]),
    ]
    for load in loads:
        load.start()

    pl.semaphore_wait(barrier, 2 + jnp.where(has_p, 1, 0) + jnp.where(has_m, 1, 0))

    def send_zm(g):
        @pl.when(has_m)
        def _():
            for kv in range(2):
                along_z(TO_ZM, g, kv).start()

    def send_zp(g):
        @pl.when(has_p)
        def _():
            for kv in range(2):
                along_z(TO_ZP, g, kv).start()

    @pl.when(gives)
    def _():
        send_zm(0)

    send_zp(0)
    picks_to_y.start()
    to_y(0, 0).start()
    for kv in range(2):
        relayed(R_Y, kv).start()
    for kv in range(2):
        to_sib(kv).start()
    for g in range(1, count + 1):

        if g < count:

            @pl.when(gives)
            def _():
                send_zm(g)

        if g < HELD:
            send_zp(g)
        if g < count:
            to_y(0, g).start()

    @pl.when(takes)
    def _():
        for kv in range(2):
            to_sib(kv).wait_recv()
        for g in range(count + 1):
            send_zm(g)

    load_w.start()
    load_picks.wait()
    picks_to_y.wait_recv()

    ints = jnp.int32
    row_at = lax.broadcasted_iota(ints, (rows, rows), 0)
    col_at = lax.broadcasted_iota(ints, (rows, rows), 1)
    row_first = row_at < BLK
    col_first = col_at < BLK
    diagonal = row_at == col_at

    def fill(index, named, up, down, valid):
        one = jnp.where(valid, 1, 0)
        seconds = [
            jnp.where(even, named[b, up] + named[b, up + 1], named[b, down] + named[b, down + 1]) for b in range(2)
        ]
        cells = [[((2 - n) * one).astype(jnp.float32), (n * one).astype(jnp.float32)] for n in seconds]
        mult[index] = jnp.where(
            row_first,
            jnp.where(col_first, cells[0][0], cells[0][1]),
            jnp.where(col_first, cells[1][0], cells[1][1]),
        )

    near_valid = gives | has_p
    fill(F_ZP, picks, 6, 2, has_p)
    fill(F_ZM, picks, 2, 6, has_m)
    fill(F_OWN, picks_y, 0, 4, True)
    fill(F_ZPY, picks_y, 4, 0, has_p)
    fill(F_YN, picks, 4, 0, True)
    fill(F_DG, picks, 0, 4, has_m)
    over_valid = takes | has_m
    mult[F_XR] = jnp.full((rows, rows), jnp.where(over_valid, 1.0, 0.0), jnp.float32)
    mult[F_NEAR] = jnp.full((rows, rows), jnp.where(near_valid, 1.0, 0.0), jnp.float32)

    def clear(ref, index):
        ref[index * rows : (index + 1) * rows] = jnp.zeros((rows, ref.shape[1]), ref.dtype)

    @pl.when(jnp.logical_not(has_p))
    def _():
        clear(vbuf, ZP)

    @pl.when(jnp.logical_not(has_m))
    def _():
        clear(vbuf, ZM)
        clear(vrel, DG)

    @pl.when(jnp.logical_not(near_valid))
    def _():
        clear(vbuf, XF)

    @pl.when(jnp.logical_not(over_valid))
    def _():
        clear(vrel, XR)

    near = pl.ds(pl.multiple_of(jnp.where(gives, SIB, XF) * rows, rows), rows)

    def weigh(query, head, parts):
        columns = slice(head * HEAD_DIM, (head + 1) * HEAD_DIM)
        pieces = []
        for k_from, _, factors in parts:
            scores = lax.dot_general(
                query[:, columns],
                k_from[...],
                (((1,), (1,)), ((), ())),
                preferred_element_type=jnp.float32,
            )
            for i, factor in enumerate(factors):
                piece = scores[:, i * rows : (i + 1) * rows]
                if factor is not None:
                    piece = jnp.where(mult[factor] > 0, piece, NEG)
                pieces.append((piece, factor))
        high = functools.reduce(jnp.maximum, [piece for piece, _ in pieces])
        high = jnp.broadcast_to(jnp.max(high, axis=1, keepdims=True), high.shape)
        weights = []
        for piece, factor in pieces:
            weight = jnp.exp2((piece - high) * EXP_SCALE)
            if factor is not None:
                weight = weight * mult[factor]
            weights.append(weight)
        summed = functools.reduce(jnp.add, weights)
        summed = jnp.broadcast_to(jnp.sum(summed, axis=1, keepdims=True), summed.shape)
        return high * EXP_SCALE, summed, [weight.astype(jnp.bfloat16) for weight in weights]

    def gather(weights, parts):
        mixed = None
        for _, v_from, factors in parts:
            now, weights = weights[: len(factors)], weights[len(factors) :]
            now = jnp.concatenate(now, axis=1)
            term = jnp.dot(now, v_from[...], preferred_element_type=jnp.float32)
            mixed = term if mixed is None else mixed + term
        return mixed

    def held(where, head, factors):
        columns = pl.ds(head * HEAD_DIM, HEAD_DIM)
        return kbuf.at[where, columns], vbuf.at[where, columns], factors

    def help_parts(head):
        return held(near, head, (F_NEAR,)), held(pl.ds(OWN * rows, 2 * rows), head, (F_OWN, F_ZPY))

    def heads_of(g):
        return range(FIRST[g], FIRST[g] + SPANS[g])

    def help_weigh(g):
        found = [weigh(qy, head, help_parts(head)) for head in heads_of(g)]
        for j, (high, summed, _) in enumerate(found):
            size = high + jnp.log2(summed)
            give_l[g, j : j + 1] = jnp.sum(jnp.where(diagonal, size, 0.0), axis=0, keepdims=True)
        return found

    def help_gather(g, found):
        for head, (_, summed, weights) in zip(heads_of(g), found):
            columns = slice(head * HEAD_DIM, (head + 1) * HEAD_DIM)
            mixed = gather(weights, help_parts(head))
            give_o[:, columns] = (mixed / summed).astype(give_o.dtype)

    def near_part(head):
        return held(pl.ds(SIB * rows, 4 * rows), head, (None, None, F_ZP, F_ZM))

    def local_weigh(g):
        found = [weigh(qv, head, (near_part(head),)) for head in heads_of(g)]
        for head, (high, summed, _) in zip(heads_of(g), found):
            top[head], tot[head] = high, summed
        return [weights for _, _, weights in found]

    def local_gather(g, found):
        for head, weights in zip(heads_of(g), found):
            acc[head] = gather(weights, (near_part(head),))

    def relayed_parts(head):
        mine = pl.ds((head - FIRST[count]) * HEAD_DIM, HEAD_DIM)
        return near_part(head), (krel.at[:, mine], vrel.at[:, mine], (F_YN, F_DG, F_XR))

    def relayed_ready(kv):
        @pl.when(has_p)
        def _():
            along_z(TO_ZM, count, kv).wait_recv()

        below_ready(count, kv)

        @pl.when(over_valid)
        def _():
            relayed(R_SIB, kv).wait_recv()

    def relayed_weigh():
        return [weigh(qv, head, relayed_parts(head)) for head in heads_of(count)]

    def relayed_gather(found):
        for head, (_, summed, weights) in zip(heads_of(count), found):
            columns = slice(head * HEAD_DIM, (head + 1) * HEAD_DIM)
            mixed = gather(weights, relayed_parts(head))
            mixed_heads[:, columns] = (mixed / summed).astype(mixed_heads.dtype)

    def returned(g):
        for kind in (1, 2):
            to_y(kind, g).wait_recv()

    def merge_group(g):
        for j in range(GROUPS[g]):
            head = FIRST[g] + j
            columns = slice(head * HEAD_DIM, (head + 1) * HEAD_DIM)
            size = jnp.broadcast_to(take_l[g, j : j + 1], (rows, rows))
            size = jnp.sum(jnp.where(diagonal, size, 0.0), axis=1, keepdims=True)
            size = jnp.broadcast_to(size, (rows, rows))
            high = jnp.maximum(top[head], size)
            mine = jnp.exp2(top[head] - high)
            theirs = jnp.exp2(size - high)
            mixed = acc[head] * mine + take_o[:, columns].astype(jnp.float32) * theirs
            mixed_heads[:, columns] = (mixed / (tot[head] * mine + theirs)).astype(mixed_heads.dtype)

    for load in loads:
        load.wait()

    @pl.when(gives)
    def _():
        for kv in range(2):
            to_sib(kv).wait_recv()
    def relay():
        for kv in range(2):
            relayed(R_Y, kv).wait_recv()

        @pl.when(has_p)
        def _():
            for kv in range(2):
                relayed(R_Z, kv).start()

        for g in range(HELD, count + 1):
            send_zp(g)

        @pl.when(gives)
        def _():
            for kv in range(2):
                relayed(R_SIB, kv).start()

    def above_ready(g, kv):
        @pl.when(has_p)
        def _():
            along_z(TO_ZM, g, kv).wait_recv()

        @pl.when(has_p & gives)
        def _():
            along_z(HAND, g, kv).start()

    def handed(g, kv):
        @pl.when(has_p & takes)
        def _():
            along_z(HAND, g, kv).wait_recv()

    def below_ready(g, kv):
        @pl.when(has_m)
        def _():
            along_z(TO_ZP, g, kv).wait_recv()

    def project(first, end):
        rows_of = slice(FIRST[first] * HEAD_DIM, (FIRST[end - 1] + SPANS[end - 1]) * HEAD_DIM)
        return jnp.dot(mixed_heads[:, rows_of], wv[rows_of], preferred_element_type=jnp.float32)

    def give(g):
        for kind in (1, 2):
            to_y(kind, g).start()

    final = count - 1
    for g in range(count):
        if g == final:
            load_w.wait()
            for done in range(EARLY):
                returned(done)
            for done in range(EARLY):
                merge_group(done)
            projected[...] = project(0, EARLY)
        if g > 0:
            below_ready(g - 1, 1)
            local_gather(g - 1, nearby)
        if g == final:

            @pl.when(gives)
            def _():
                send_zm(count)

        above_ready(g, 0)
        handed(g, 0)
        if g < final:
            to_y(0, g).wait_recv()
            found = help_weigh(g)
        else:

            @pl.when(has_p)
            def _():
                to_y(0, final).wait_recv()
                for j, (_, summed, weights) in enumerate(help_weigh(final)):
                    kept_sum[j] = summed
                    for i, weight in enumerate(weights):
                        kept[j, i] = weight

        below_ready(g, 0)
        nearby = local_weigh(g)
        above_ready(g, 1)
        handed(g, 1)
        if g < final:
            help_gather(g, found)
            give(g)
        else:

            @pl.when(has_p)
            def _():
                help_gather(final, [(None, kept_sum[j], [kept[j, i] for i in range(3)]) for j in range(GROUPS[final])])
                give(final)

        if g == 0:
            relay()
        if g == 1:

            @pl.when(jnp.logical_not(has_p))
            def _():
                to_y(0, final).wait_recv()
                help_gather(final, help_weigh(final))
                give(final)

    below_ready(final, 1)
    for g in range(EARLY, final):
        returned(g)
    local_gather(final, nearby)
    for g in range(EARLY, final):
        merge_group(g)
    projected[...] += project(EARLY, final)

    @pl.when(has_m)
    def _():
        for kv in range(2):
            relayed(R_Z, kv).wait_recv()

    @pl.when(has_m & takes)
    def _():
        for kv in range(2):
            relayed(R_SIB, kv, DG).start()

    relayed_ready(0)
    found = relayed_weigh()
    relayed_ready(1)

    def sends_done(first, end):
        for kind, sent in ((TO_ZP, has_p), (TO_ZM, has_m)):

            @pl.when(sent)
            def _():
                for g in range(first, end):
                    for kv in range(2):
                        along_z(kind, g, kv).wait_send()

    picks_to_y.wait_send()
    for kv in range(2):
        to_sib(kv).wait_send()
        relayed(R_Y, kv).wait_send()
    for g in range(count):
        for kind in range(3 if g < count - 1 else 1):
            to_y(kind, g).wait_send()

    @pl.when(has_p & gives)
    def _():
        for g in range(count - 1):
            for kv in range(2):
                along_z(HAND, g, kv).wait_send()

    sends_done(0, 1)

    returned(final)
    relayed_gather(found)
    merge_group(final)
    out[...] = (projected[...] + project(count - 1, count + 1)).astype(out.dtype)
    for kind in (1, 2):
        to_y(kind, count - 1).wait_send()
    sends_done(1, count + 1)

    @pl.when(has_p)
    def _():
        for kv in range(2):
            relayed(R_Z, kv).wait_send()

    @pl.when(gives | has_m)
    def _():
        for kv in range(2):
            relayed(R_SIB, kv).wait_send()

    @pl.when(has_p & gives)
    def _():
        for kv in range(2):
            along_z(HAND, count - 1, kv).wait_send()


def attention(devices, queries, keys, values, far_picks, out_weight):
    rows, width = queries.shape
    count = len(GROUPS)
    in_hbm = pl.BlockSpec(memory_space=pltpu.HBM)
    per_head = pltpu.VMEM((HEADS, rows, HEAD_DIM), jnp.float32)
    wide = pltpu.VMEM((rows, width), jnp.bfloat16)
    sizes = pltpu.VMEM((count, 8, rows), jnp.float32)
    over = pltpu.VMEM((3 * rows, RELAYED * HEAD_DIM), jnp.bfloat16)
    dma = pltpu.SemaphoreType.DMA
    return pl.pallas_call(
        functools.partial(kernel, devices),
        out_shape=jax.ShapeDtypeStruct((rows, width), jnp.bfloat16),
        in_specs=[in_hbm] * 5,
        out_specs=pl.BlockSpec(memory_space=pltpu.VMEM),
        scratch_shapes=[
            pltpu.SMEM(far_picks.shape, jnp.int32),
            pltpu.SMEM(far_picks.shape, jnp.int32),
            wide,
            wide,
            pltpu.VMEM(out_weight.shape, jnp.bfloat16),
            pltpu.VMEM((5 * rows, width), jnp.bfloat16),
            pltpu.VMEM((5 * rows, width), jnp.bfloat16),
            over,
            over,
            pltpu.VMEM((8, rows, rows), jnp.float32),
            per_head,
            per_head,
            per_head,
            wide,
            sizes,
            wide,
            sizes,
            wide,
            pltpu.VMEM((rows, width), jnp.float32),
            pltpu.VMEM((GROUPS[-1], 3, rows, rows), jnp.bfloat16),
            pltpu.VMEM((GROUPS[-1], rows, HEAD_DIM), jnp.float32),
            dma((5,)),
            dma((3, count + 1, 2)),
            dma((3, count + 1, 2)),
            dma((2,)),
            dma((2,)),
            dma((3, count)),
            dma((3, count)),
            dma,
            dma,
            dma((3, 2)),
            dma((3, 2)),
        ],
        compiler_params=pltpu.CompilerParams(
            collective_id=0, has_side_effects=True, vmem_limit_bytes=56_000_000
        ),
        name="helper_attention",
    )(*(pltpu.with_memory_space_constraint(x, pltpu.HBM) for x in (far_picks, queries, keys, values, out_weight)))


def solution(mesh):
    devices = mesh.shape["tm"]

    def body(queries, keys, values, far_picks, out_weight):
        return attention(devices, queries, keys, values, far_picks, out_weight)

    placed = (
        P(("vid", "tm"), None),
        P(("vid", "tm"), None),
        P(("vid", "tm"), None),
        P(("vid", "tm"), None),
        P(),
    )
    return jax.shard_map(
        body, mesh=mesh, in_specs=placed, out_specs=P(("vid", "tm"), None), check_vma=False
    )
```

```python
import functools
import math

import jax
import jax.numpy as jnp
from jax import lax
from jax.experimental import pallas as pl
from jax.experimental.pallas import tpu as pltpu
from jax.sharding import PartitionSpec as P

HEADS = 12
HEAD_DIM = 128
BLK = 64
NEG = -1e30
EXP_SCALE = HEAD_DIM ** (-0.5) * math.log2(math.e)
XF, SIB, OWN, ZP, ZM = range(5)
TO_ZP, TO_ZM, HAND = range(3)
YN, DG, XR = range(3)
R_Y, R_Z, R_SIB = range(3)
F_ZP, F_ZM, F_OWN, F_ZPY, F_NEAR, F_YN, F_DG, F_XR = range(8)
MESH = pl.DeviceIdType.MESH
GROUPS = (4, 3, 2, 2)
RELAYED = 1
SPANS = GROUPS + (RELAYED,)
FIRST = tuple(sum(SPANS[:g]) for g in range(len(SPANS)))
HELD = 4
EARLY = 1


def kernel(
    devices,
    picks_hbm,
    q_hbm,
    k_hbm,
    v_hbm,
    w_hbm,
    out,
    picks,
    picks_y,
    qv,
    qy,
    wv,
    kbuf,
    vbuf,
    krel,
    vrel,
    mult,
    top,
    tot,
    acc,
    give_o,
    give_l,
    take_o,
    take_l,
    mixed_heads,
    projected,
    kept,
    kept_sum,
    load_sem,
    send_z,
    recv_z,
    send_sib,
    recv_sib,
    send_y,
    recv_y,
    send_p,
    recv_p,
    send_r,
    recv_r,
):
    rows = q_hbm.shape[0]
    chips = devices // 2
    count = len(GROUPS)
    p = lax.axis_index("tm")
    chip = p // 2
    core = p % 2
    even = chip % 2 == 0
    step = jnp.where(even, 1, -1)
    has_p = (chip + 2 * step >= 0) & (chip + 2 * step < chips)
    has_m = (chip - 2 * step >= 0) & (chip - 2 * step < chips)
    gives = (core + chip) % 2 == 0
    takes = jnp.logical_not(gives)

    sib = p + 1 - 2 * core
    y_dev = p + 2 * step
    zp_dev = p + 4 * step
    zm_dev = p - 4 * step
    bufs = (kbuf, vbuf)
    hbms = (k_hbm, v_hbm)
    rels = (krel, vrel)

    def columns_of(g):
        return pl.ds(FIRST[g] * HEAD_DIM, SPANS[g] * HEAD_DIM)

    def slot(index):
        return pl.ds(index * rows, rows)

    def remote(src, dst, send, recv, dev):
        return pltpu.make_async_remote_copy(
            src_ref=src, dst_ref=dst, send_sem=send, recv_sem=recv, device_id={"tm": dev}, device_id_type=MESH
        )

    def along_z(kind, g, kv):
        dst, dev = ((ZM, zp_dev), (ZP, zm_dev), (XF, sib))[kind]
        columns = columns_of(g)
        src = bufs[kv].at[slot(ZP), columns] if kind == HAND else hbms[kv].at[:, columns]
        where = (kind, g, kv)
        return remote(src, bufs[kv].at[slot(dst), columns], send_z.at[where], recv_z.at[where], dev)

    def to_sib(kv):
        return remote(hbms[kv], bufs[kv].at[slot(SIB)], send_sib.at[kv], recv_sib.at[kv], sib)

    def to_y(kind, g):
        columns = columns_of(g)
        src, dst = (
            (q_hbm.at[:, columns], qy.at[:, columns]),
            (give_o.at[:, columns], take_o.at[:, columns]),
            (give_l.at[g], take_l.at[g]),
        )[kind]
        return remote(src, dst, send_y.at[kind, g], recv_y.at[kind, g], y_dev)

    def relayed(kind, kv, given=YN):
        src = hbms[kv].at[:, columns_of(count)] if kind == R_Y else rels[kv].at[slot(given)]
        dst, dev = ((YN, y_dev), (DG, zp_dev), (XR, sib))[kind]
        return remote(src, rels[kv].at[slot(dst)], send_r.at[kind, kv], recv_r.at[kind, kv], dev)

    picks_to_y = remote(picks_hbm, picks_y, send_p, recv_p, y_dev)
    load_w = pltpu.make_async_copy(w_hbm, wv, load_sem.at[4])
    load_picks = pltpu.make_async_copy(picks_hbm, picks, load_sem.at[3])
    barrier = pltpu.get_barrier_semaphore()

    def greet(dev):
        pl.semaphore_signal(barrier, inc=1, device_id={"tm": dev}, device_id_type=MESH)

    greet(sib)
    greet(y_dev)

    @pl.when(has_p)
    def _():
        greet(zp_dev)

    @pl.when(has_m)
    def _():
        greet(zm_dev)

    load_picks.start()
    loads = [
        pltpu.make_async_copy(q_hbm, qv, load_sem.at[0]),
        pltpu.make_async_copy(k_hbm, kbuf.at[slot(OWN)], load_sem.at[1]),
        pltpu.make_async_copy(v_hbm, vbuf.at[slot(OWN)], load_sem.at[2]),
    ]
    for load in loads:
        load.start()

    pl.semaphore_wait(barrier, 2 + jnp.where(has_p, 1, 0) + jnp.where(has_m, 1, 0))

    def send_zm(g):
        @pl.when(has_m)
        def _():
            for kv in range(2):
                along_z(TO_ZM, g, kv).start()

    def send_zp(g):
        @pl.when(has_p)
        def _():
            for kv in range(2):
                along_z(TO_ZP, g, kv).start()

    @pl.when(gives)
    def _():
        send_zm(0)

    send_zp(0)
    picks_to_y.start()
    to_y(0, 0).start()
    for kv in range(2):
        relayed(R_Y, kv).start()
    for kv in range(2):
        to_sib(kv).start()
    for g in range(1, count + 1):

        if g < count:

            @pl.when(gives)
            def _():
                send_zm(g)

        if g < HELD:
            send_zp(g)
        if g < count:
            to_y(0, g).start()

    @pl.when(takes)
    def _():
        for kv in range(2):
            to_sib(kv).wait_recv()
        for g in range(count + 1):
            send_zm(g)

    load_w.start()
    load_picks.wait()
    picks_to_y.wait_recv()

    ints = jnp.int32
    row_at = lax.broadcasted_iota(ints, (rows, rows), 0)
    col_at = lax.broadcasted_iota(ints, (rows, rows), 1)
    row_first = row_at < BLK
    col_first = col_at < BLK
    diagonal = row_at == col_at

    def fill(index, named, up, down, valid):
        one = jnp.where(valid, 1, 0)
        seconds = [
            jnp.where(even, named[b, up] + named[b, up + 1], named[b, down] + named[b, down + 1]) for b in range(2)
        ]
        cells = [[((2 - n) * one).astype(jnp.float32), (n * one).astype(jnp.float32)] for n in seconds]
        mult[index] = jnp.where(
            row_first,
            jnp.where(col_first, cells[0][0], cells[0][1]),
            jnp.where(col_first, cells[1][0], cells[1][1]),
        )

    near_valid = gives | has_p
    fill(F_ZP, picks, 6, 2, has_p)
    fill(F_ZM, picks, 2, 6, has_m)
    fill(F_OWN, picks_y, 0, 4, True)
    fill(F_ZPY, picks_y, 4, 0, has_p)
    fill(F_YN, picks, 4, 0, True)
    fill(F_DG, picks, 0, 4, has_m)
    over_valid = takes | has_m
    mult[F_XR] = jnp.full((rows, rows), jnp.where(over_valid, 1.0, 0.0), jnp.float32)
    mult[F_NEAR] = jnp.full((rows, rows), jnp.where(near_valid, 1.0, 0.0), jnp.float32)

    def clear(ref, index):
        ref[index * rows : (index + 1) * rows] = jnp.zeros((rows, ref.shape[1]), ref.dtype)

    @pl.when(jnp.logical_not(has_p))
    def _():
        clear(vbuf, ZP)

    @pl.when(jnp.logical_not(has_m))
    def _():
        clear(vbuf, ZM)
        clear(vrel, DG)

    @pl.when(jnp.logical_not(near_valid))
    def _():
        clear(vbuf, XF)

    @pl.when(jnp.logical_not(over_valid))
    def _():
        clear(vrel, XR)

    near = pl.ds(pl.multiple_of(jnp.where(gives, SIB, XF) * rows, rows), rows)

    def weigh(query, head, parts):
        columns = slice(head * HEAD_DIM, (head + 1) * HEAD_DIM)
        pieces = []
        for k_from, _, factors in parts:
            scores = lax.dot_general(
                query[:, columns],
                k_from[...],
                (((1,), (1,)), ((), ())),
                preferred_element_type=jnp.float32,
            )
            for i, factor in enumerate(factors):
                piece = scores[:, i * rows : (i + 1) * rows]
                if factor is not None:
                    piece = jnp.where(mult[factor] > 0, piece, NEG)
                pieces.append((piece, factor))
        high = functools.reduce(jnp.maximum, [piece for piece, _ in pieces])
        high = jnp.broadcast_to(jnp.max(high, axis=1, keepdims=True), high.shape)
        weights = []
        for piece, factor in pieces:
            weight = jnp.exp2((piece - high) * EXP_SCALE)
            if factor is not None:
                weight = weight * mult[factor]
            weights.append(weight)
        summed = functools.reduce(jnp.add, weights)
        summed = jnp.broadcast_to(jnp.sum(summed, axis=1, keepdims=True), summed.shape)
        return high * EXP_SCALE, summed, [weight.astype(jnp.bfloat16) for weight in weights]

    def gather(weights, parts):
        mixed = None
        for _, v_from, factors in parts:
            now, weights = weights[: len(factors)], weights[len(factors) :]
            now = jnp.concatenate(now, axis=1)
            term = jnp.dot(now, v_from[...], preferred_element_type=jnp.float32)
            mixed = term if mixed is None else mixed + term
        return mixed

    def held(where, head, factors):
        columns = pl.ds(head * HEAD_DIM, HEAD_DIM)
        return kbuf.at[where, columns], vbuf.at[where, columns], factors

    def help_parts(head):
        return held(near, head, (F_NEAR,)), held(pl.ds(OWN * rows, 2 * rows), head, (F_OWN, F_ZPY))

    def heads_of(g):
        return range(FIRST[g], FIRST[g] + SPANS[g])

    def help_weigh(g):
        found = [weigh(qy, head, help_parts(head)) for head in heads_of(g)]
        for j, (high, summed, _) in enumerate(found):
            size = high + jnp.log2(summed)
            give_l[g, j : j + 1] = jnp.sum(jnp.where(diagonal, size, 0.0), axis=0, keepdims=True)
        return found

    def help_gather(g, found):
        for head, (_, summed, weights) in zip(heads_of(g), found):
            columns = slice(head * HEAD_DIM, (head + 1) * HEAD_DIM)
            mixed = gather(weights, help_parts(head))
            give_o[:, columns] = (mixed / summed).astype(give_o.dtype)

    def near_part(head):
        return held(pl.ds(SIB * rows, 4 * rows), head, (None, None, F_ZP, F_ZM))

    def local_weigh(g):
        found = [weigh(qv, head, (near_part(head),)) for head in heads_of(g)]
        for head, (high, summed, _) in zip(heads_of(g), found):
            top[head], tot[head] = high, summed
        return [weights for _, _, weights in found]

    def local_gather(g, found):
        for head, weights in zip(heads_of(g), found):
            acc[head] = gather(weights, (near_part(head),))

    def relayed_parts(head):
        mine = pl.ds((head - FIRST[count]) * HEAD_DIM, HEAD_DIM)
        return near_part(head), (krel.at[:, mine], vrel.at[:, mine], (F_YN, F_DG, F_XR))

    def relayed_ready(kv):
        @pl.when(has_p)
        def _():
            along_z(TO_ZM, count, kv).wait_recv()

        below_ready(count, kv)

        @pl.when(over_valid)
        def _():
            relayed(R_SIB, kv).wait_recv()

    def relayed_weigh():
        return [weigh(qv, head, relayed_parts(head)) for head in heads_of(count)]

    def relayed_gather(found):
        for head, (_, summed, weights) in zip(heads_of(count), found):
            columns = slice(head * HEAD_DIM, (head + 1) * HEAD_DIM)
            mixed = gather(weights, relayed_parts(head))
            mixed_heads[:, columns] = (mixed / summed).astype(mixed_heads.dtype)

    def returned(g):
        for kind in (1, 2):
            to_y(kind, g).wait_recv()

    def merge_group(g):
        for j in range(GROUPS[g]):
            head = FIRST[g] + j
            columns = slice(head * HEAD_DIM, (head + 1) * HEAD_DIM)
            size = jnp.broadcast_to(take_l[g, j : j + 1], (rows, rows))
            size = jnp.sum(jnp.where(diagonal, size, 0.0), axis=1, keepdims=True)
            size = jnp.broadcast_to(size, (rows, rows))
            high = jnp.maximum(top[head], size)
            mine = jnp.exp2(top[head] - high)
            theirs = jnp.exp2(size - high)
            mixed = acc[head] * mine + take_o[:, columns].astype(jnp.float32) * theirs
            mixed_heads[:, columns] = (mixed / (tot[head] * mine + theirs)).astype(mixed_heads.dtype)

    for load in loads:
        load.wait()

    @pl.when(gives)
    def _():
        for kv in range(2):
            to_sib(kv).wait_recv()
    def relay():
        for kv in range(2):
            relayed(R_Y, kv).wait_recv()

        @pl.when(has_p)
        def _():
            for kv in range(2):
                relayed(R_Z, kv).start()

        for g in range(HELD, count + 1):
            send_zp(g)

        @pl.when(gives)
        def _():
            for kv in range(2):
                relayed(R_SIB, kv).start()

    def above_ready(g, kv):
        @pl.when(has_p)
        def _():
            along_z(TO_ZM, g, kv).wait_recv()

        @pl.when(has_p & gives)
        def _():
            along_z(HAND, g, kv).start()

    def handed(g, kv):
        @pl.when(has_p & takes)
        def _():
            along_z(HAND, g, kv).wait_recv()

    def below_ready(g, kv):
        @pl.when(has_m)
        def _():
            along_z(TO_ZP, g, kv).wait_recv()

    def project(first, end):
        rows_of = slice(FIRST[first] * HEAD_DIM, (FIRST[end - 1] + SPANS[end - 1]) * HEAD_DIM)
        return jnp.dot(mixed_heads[:, rows_of], wv[rows_of], preferred_element_type=jnp.float32)

    def give(g):
        for kind in (1, 2):
            to_y(kind, g).start()

    final = count - 1
    for g in range(count):
        if g == final:
            load_w.wait()
            for done in range(EARLY):
                returned(done)
            for done in range(EARLY):
                merge_group(done)
            projected[...] = project(0, EARLY)
        if g > 0:
            below_ready(g - 1, 1)
            local_gather(g - 1, nearby)
        if g == final:

            @pl.when(gives)
            def _():
                send_zm(count)

        above_ready(g, 0)
        handed(g, 0)
        if g < final:
            to_y(0, g).wait_recv()
            found = help_weigh(g)
        else:

            @pl.when(has_p)
            def _():
                to_y(0, final).wait_recv()
                for j, (_, summed, weights) in enumerate(help_weigh(final)):
                    kept_sum[j] = summed
                    for i, weight in enumerate(weights):
                        kept[j, i] = weight

        below_ready(g, 0)
        nearby = local_weigh(g)
        above_ready(g, 1)
        handed(g, 1)
        if g < final:
            help_gather(g, found)
            give(g)
        else:

            @pl.when(has_p)
            def _():
                help_gather(final, [(None, kept_sum[j], [kept[j, i] for i in range(3)]) for j in range(GROUPS[final])])
                give(final)

        if g == 0:
            relay()
        if g == 1:

            @pl.when(jnp.logical_not(has_p))
            def _():
                to_y(0, final).wait_recv()
                help_gather(final, help_weigh(final))
                give(final)

    below_ready(final, 1)
    for g in range(EARLY, final):
        returned(g)
    local_gather(final, nearby)
    for g in range(EARLY, final):
        merge_group(g)
    projected[...] += project(EARLY, final)

    @pl.when(has_m)
    def _():
        for kv in range(2):
            relayed(R_Z, kv).wait_recv()

    @pl.when(has_m & takes)
    def _():
        for kv in range(2):
            relayed(R_SIB, kv, DG).start()

    relayed_ready(0)
    found = relayed_weigh()
    relayed_ready(1)

    def sends_done(first, end):
        for kind, sent in ((TO_ZP, has_p), (TO_ZM, has_m)):

            @pl.when(sent)
            def _():
                for g in range(first, end):
                    for kv in range(2):
                        along_z(kind, g, kv).wait_send()

    picks_to_y.wait_send()
    for kv in range(2):
        to_sib(kv).wait_send()
        relayed(R_Y, kv).wait_send()
    for g in range(count):
        for kind in range(3 if g < count - 1 else 1):
            to_y(kind, g).wait_send()

    @pl.when(has_p & gives)
    def _():
        for g in range(count - 1):
            for kv in range(2):
                along_z(HAND, g, kv).wait_send()

    sends_done(0, 1)

    returned(final)
    relayed_gather(found)
    merge_group(final)
    out[...] = (projected[...] + project(count - 1, count + 1)).astype(out.dtype)
    for kind in (1, 2):
        to_y(kind, count - 1).wait_send()
    sends_done(1, count + 1)

    @pl.when(has_p)
    def _():
        for kv in range(2):
            relayed(R_Z, kv).wait_send()

    @pl.when(gives | has_m)
    def _():
        for kv in range(2):
            relayed(R_SIB, kv).wait_send()

    @pl.when(has_p & gives)
    def _():
        for kv in range(2):
            along_z(HAND, count - 1, kv).wait_send()


def attention(devices, queries, keys, values, far_picks, out_weight):
    rows, width = queries.shape
    count = len(GROUPS)
    in_hbm = pl.BlockSpec(memory_space=pltpu.HBM)
    per_head = pltpu.VMEM((HEADS, rows, HEAD_DIM), jnp.float32)
    wide = pltpu.VMEM((rows, width), jnp.bfloat16)
    sizes = pltpu.VMEM((count, 8, rows), jnp.float32)
    over = pltpu.VMEM((3 * rows, RELAYED * HEAD_DIM), jnp.bfloat16)
    dma = pltpu.SemaphoreType.DMA
    return pl.pallas_call(
        functools.partial(kernel, devices),
        out_shape=jax.ShapeDtypeStruct((rows, width), jnp.bfloat16),
        in_specs=[in_hbm] * 5,
        out_specs=pl.BlockSpec(memory_space=pltpu.VMEM),
        scratch_shapes=[
            pltpu.SMEM(far_picks.shape, jnp.int32),
            pltpu.SMEM(far_picks.shape, jnp.int32),
            wide,
            wide,
            pltpu.VMEM(out_weight.shape, jnp.bfloat16),
            pltpu.VMEM((5 * rows, width), jnp.bfloat16),
            pltpu.VMEM((5 * rows, width), jnp.bfloat16),
            over,
            over,
            pltpu.VMEM((8, rows, rows), jnp.float32),
            per_head,
            per_head,
            per_head,
            wide,
            sizes,
            wide,
            sizes,
            wide,
            pltpu.VMEM((rows, width), jnp.float32),
            pltpu.VMEM((GROUPS[-1], 3, rows, rows), jnp.bfloat16),
            pltpu.VMEM((GROUPS[-1], rows, HEAD_DIM), jnp.float32),
            dma((5,)),
            dma((3, count + 1, 2)),
            dma((3, count + 1, 2)),
            dma((2,)),
            dma((2,)),
            dma((3, count)),
            dma((3, count)),
            dma,
            dma,
            dma((3, 2)),
            dma((3, 2)),
        ],
        compiler_params=pltpu.CompilerParams(
            collective_id=0, has_side_effects=True, vmem_limit_bytes=56_000_000
        ),
        name="helper_attention",
    )(*(pltpu.with_memory_space_constraint(x, pltpu.HBM) for x in (far_picks, queries, keys, values, out_weight)))


def solution(mesh):
    devices = mesh.shape["tm"]

    def body(queries, keys, values, far_picks, out_weight):
        return attention(devices, queries, keys, values, far_picks, out_weight)

    placed = (
        P(("vid", "tm"), None),
        P(("vid", "tm"), None),
        P(("vid", "tm"), None),
        P(("vid", "tm"), None),
        P(),
    )
    return jax.shard_map(
        body, mesh=mesh, in_specs=placed, out_specs=P(("vid", "tm"), None), check_vma=False
    )
```
